512 devices in a mesh: tm: 8 (over x, z_hi), vert: 64 (over y, z_lo, core).
Axes of the slice: x: 4, y: 8, z: 8 (z_hi: 2, z_lo: 4; z = z_hi * 4 + z_lo), core: 2. Of those that a mesh axis runs over, the one named last changes fastest.
Arguments:
- frames: bfloat16 [16, 8192, 256], P('tm', 'vert'), may hold values from -12 to 12
- cotangent: bfloat16 [16, 8192, 256], P('tm', 'vert'), may hold values from -200 to 200
- table: int32 [8192, 7], P('vert'), may hold values from -1 to 8191, as said below
- w_conv: bfloat16 [1792, 256], replicated, may hold values from -0.125 to 0.125
- w_attn: bfloat16 [4, 256, 256], replicated, may hold values from -0.375 to 0.375
Outputs:
- grad_frames: bfloat16 [16, 8192, 256], P('tm', 'vert')
- grad_conv: bfloat16 [1792, 256], replicated
- grad_attn: bfloat16 [4, 256, 256], replicated
The draws below stay inside these ranges and needn't reach their ends.
Inputs may be any that keep to these rules, and one draw needn't show every extreme that they name: `table`: each entry of row v is -1 (an empty slot) or a vertex at most 64 places from v in the vertex order; slot 0 is v itself; some entries lie exactly 64 places away on either side.
All inputs are finite; a program needn't handle non-finite values.
Results may differ from the reference program's by a relative error of at most 0.014.
The reference program's roundings to bfloat16 on the way count: a program that leaves them out, or rounds other values in their place, can miss the bound.
Values may be sent and summed in bfloat16 or wider, within the bound.
No kernel may reach another device: no remote copies, remote signals or barrier semaphores. Data moves between devices by JAX's collectives and lax.ppermute only.
A program may use at most 64 MiB of HBM per device.

```python
import jax
import jax.numpy as jnp
from jax import lax

TF = 16
C = 256
HEADS = 8
STENCIL = 7
VP = 128
HW = 64
V = 8192


def draw_frames(key, part):
    key_base = jax.random.fold_in(key, 0)
    values = jax.random.normal(key_base, (TF, V, C), jnp.float32)
    return jnp.clip(values, -6.0, 6.0).astype(jnp.bfloat16)


def draw_cotangent(key, part):
    frame_pos = jnp.arange(TF, dtype=jnp.float32) / (TF - 1.0)
    vertex_pos = jnp.arange(V, dtype=jnp.float32) / (V - 1.0)
    level = jnp.log(4.0) * frame_pos[:, None, None] ** 4 + jnp.log(8.0) * vertex_pos[None, :, None] ** 16
    scale = jnp.exp(level)
    base = jnp.clip(jax.random.normal(key, (TF, V, C), jnp.float32), -6.0, 6.0)
    return (base * scale).astype(jnp.bfloat16)


def draw_table(key, part):
    vertex_ids = jnp.arange(V, dtype=jnp.int32)
    key_dist, key_sign, key_empty = jax.random.split(key, 3)
    distance = jax.random.randint(key_dist, (V, STENCIL - 1), 1, HW + 1)
    direction = jax.random.randint(key_sign, (V, STENCIL - 1), 0, 2) * 2 - 1
    offsets = distance * direction
    marked = vertex_ids % 7 == 0
    offsets = offsets.at[:, 0].set(jnp.where(marked, HW, offsets[:, 0]))
    offsets = offsets.at[:, 1].set(jnp.where(marked, -HW, offsets[:, 1]))
    others = vertex_ids[:, None] + offsets
    others = jnp.where((others < 0) | (others >= V), -1, others)
    sparse = (jax.random.randint(key_empty, (V,), 0, 64) == 0) | (vertex_ids == 0)
    others = others.at[:, -1].set(jnp.where(sparse, -1, others[:, -1]))
    return jnp.concatenate([vertex_ids[:, None], others], axis=1).astype(jnp.int32)


def normal_values(key, dims, scale, limit, held_as=jnp.bfloat16):
    entries = jax.random.normal(key, dims, jnp.float32) * scale
    return jnp.minimum(jnp.maximum(entries, -limit), limit).astype(held_as)


def setup_inputs(seed: int = 0) -> dict:
    arg_keys = jax.random.split(jax.random.key(seed), 6)
    frames = draw_frames(jax.random.fold_in(arg_keys[5], 71), 0)
    cotangent = draw_cotangent(jax.random.fold_in(arg_keys[5], 71), 0)
    table = draw_table(jax.random.fold_in(arg_keys[5], 71), 0)
    w_conv = normal_values(arg_keys[3], (STENCIL * C, C), (STENCIL * C) ** -0.5, 0.125)
    w_attn = normal_values(arg_keys[4], (4, C, C), C ** -0.5, 0.375)
    return {"frames": frames, "cotangent": cotangent, "table": table, "w_conv": w_conv, "w_attn": w_attn}


def frame_attention(query_rows, key_rows, value_rows, grad_out):
    frames_q, verts, width = query_rows.shape
    head_dim = width // HEADS
    scaling = head_dim ** -0.5
    query_heads = query_rows.reshape(frames_q, verts, HEADS, head_dim).astype(jnp.float32)
    key_heads = key_rows.reshape(-1, verts, HEADS, head_dim).astype(jnp.float32)
    value_heads = value_rows.reshape(-1, verts, HEADS, head_dim).astype(jnp.float32)
    grad_heads = grad_out.reshape(frames_q, verts, HEADS, head_dim).astype(jnp.float32)
    scores = jnp.einsum("frhd,grhd->rhfg", query_heads, key_heads) * scaling
    top_score = jnp.max(scores, axis=-1, keepdims=True)
    expo = jnp.exp(scores - top_score)
    probs = expo / jnp.sum(expo, axis=-1, keepdims=True)
    probs_b = probs.astype(jnp.bfloat16).astype(jnp.float32)
    attended = jnp.einsum("rhfg,grhd->frhd", probs_b, value_heads).astype(jnp.bfloat16)
    grad_value = jnp.einsum("rhfg,frhd->grhd", probs_b, grad_heads).astype(jnp.bfloat16)
    grad_probs = jnp.einsum("frhd,grhd->rhfg", grad_heads, value_heads)
    inner_sum = jnp.sum(probs * grad_probs, axis=-1, keepdims=True)
    grad_scores = (scaling * probs * (grad_probs - inner_sum)).astype(jnp.bfloat16).astype(jnp.float32)
    grad_query = jnp.einsum("rhfg,grhd->frhd", grad_scores, key_heads).astype(jnp.bfloat16)
    grad_key = jnp.einsum("rhfg,frhd->grhd", grad_scores, query_heads).astype(jnp.bfloat16)
    return (attended.reshape(frames_q, verts, width), grad_query.reshape(frames_q, verts, width),
            grad_key.reshape(-1, verts, width), grad_value.reshape(-1, verts, width))


def reference(frames, cotangent, table, w_conv, w_attn):
    flat_index = jnp.where(table < 0, V, table).astype(jnp.int32).reshape(-1)

    def conv_forward(frame):
        padded = jnp.concatenate([frame, jnp.zeros((1, C), jnp.bfloat16)], axis=0)
        gathered = jnp.take(padded, flat_index, axis=0).reshape(V, STENCIL * C)
        conv_pre = jnp.dot(gathered, w_conv, preferred_element_type=jnp.float32)
        return gathered, conv_pre

    def hidden_of(frame):
        gathered, conv_pre = conv_forward(frame)
        return (frame.astype(jnp.float32) + conv_pre * jax.nn.sigmoid(conv_pre)).astype(jnp.bfloat16)

    hidden = lax.map(hidden_of, frames)
    blocks = V // VP
    hidden_blocks = hidden.reshape(TF, blocks, VP, C).transpose(1, 0, 2, 3)
    grad_blocks = cotangent.reshape(TF, blocks, VP, C).transpose(1, 0, 2, 3)

    def attn_block(carry, pair):
        hidden_block, grad_block = pair
        hidden_rows = hidden_block.reshape(-1, C)
        grad_rows = grad_block.reshape(-1, C)
        query_rows = jnp.dot(hidden_rows, w_attn[0], preferred_element_type=jnp.float32).astype(jnp.bfloat16)
        key_rows = jnp.dot(hidden_rows, w_attn[1], preferred_element_type=jnp.float32).astype(jnp.bfloat16)
        value_rows = jnp.dot(hidden_rows, w_attn[2], preferred_element_type=jnp.float32).astype(jnp.bfloat16)
        grad_out = jnp.dot(grad_rows, w_attn[3].T, preferred_element_type=jnp.float32).astype(jnp.bfloat16)
        shape3 = (TF, VP, C)
        attended, grad_query, grad_key, grad_value = frame_attention(
            query_rows.reshape(shape3), key_rows.reshape(shape3), value_rows.reshape(shape3), grad_out.reshape(shape3))
        grad_query = grad_query.reshape(-1, C)
        grad_key = grad_key.reshape(-1, C)
        grad_value = grad_value.reshape(-1, C)
        grad_hidden = (grad_rows.astype(jnp.float32)
                       + jnp.dot(grad_query, w_attn[0].T, preferred_element_type=jnp.float32)
                       + jnp.dot(grad_key, w_attn[1].T, preferred_element_type=jnp.float32)
                       + jnp.dot(grad_value, w_attn[2].T, preferred_element_type=jnp.float32)).astype(jnp.bfloat16)
        parts = jnp.stack([
            jnp.dot(hidden_rows.T, grad_query, preferred_element_type=jnp.float32),
            jnp.dot(hidden_rows.T, grad_key, preferred_element_type=jnp.float32),
            jnp.dot(hidden_rows.T, grad_value, preferred_element_type=jnp.float32),
            jnp.dot(attended.reshape(-1, C).T, grad_rows, preferred_element_type=jnp.float32)])
        return carry + parts, grad_hidden.reshape(shape3)

    grad_attn, grad_hidden_blocks = lax.scan(attn_block, jnp.zeros((4, C, C), jnp.float32), (hidden_blocks, grad_blocks))
    grad_hidden = grad_hidden_blocks.transpose(1, 0, 2, 3).reshape(TF, V, C)

    def conv_back(carry, pair):
        frame, grad_frame = pair
        gathered, conv_pre = conv_forward(frame)
        gate_sig = jax.nn.sigmoid(conv_pre)
        grad_pre = (grad_frame.astype(jnp.float32) * gate_sig * (1.0 + conv_pre * (1.0 - gate_sig))).astype(jnp.bfloat16)
        total = carry + jnp.dot(gathered.T, grad_pre, preferred_element_type=jnp.float32)
        grad_gathered = jnp.dot(grad_pre, w_conv.T, preferred_element_type=jnp.float32).reshape(V * STENCIL, C)
        spread = jnp.zeros((V + 1, C), jnp.float32).at[flat_index].add(grad_gathered)
        result = (grad_frame.astype(jnp.float32) + spread[:V]).astype(jnp.bfloat16)
        return total, result

    grad_conv, grad_frames = lax.scan(conv_back, jnp.zeros((STENCIL * C, C), jnp.float32), (frames, grad_hidden))
    scaling = (TF * V) ** -0.5
    return grad_frames, (grad_conv * scaling).astype(jnp.bfloat16), (grad_attn * scaling).astype(jnp.bfloat16)
```

```python
import functools
import math

import jax
import jax.numpy as jnp
from jax import lax
from jax.experimental import pallas as pl
from jax.experimental.pallas import tpu as pltpu
from jax.sharding import PartitionSpec as P

TF = 16
HEADS = 8
HW = 64
BF = jnp.bfloat16
F32 = jnp.float32


def mm(left, right):
    return jnp.dot(left, right, preferred_element_type=F32)


def mm_nt(left, right):
    return lax.dot_general(left, right, (((1,), (1,)), ((), ())), preferred_element_type=F32)


def mm_tn(left, right):
    return lax.dot_general(left, right, (((0,), (0,)), ((), ())), preferred_element_type=F32)


def slot_columns(table, patch):
    rows = lax.broadcasted_iota(jnp.int32, table.shape, 0)
    return jnp.where(table < 0, -1, table - table[:, 0:1] + rows + HW)


def conv_forward_kernel(
    frames_ref, cot_ref, low_ref, high_ref, table_ref, w_ref, sent_ref, pre_ref, gathered_ref
):
    frames_here, patch, width = frames_ref.shape
    stencil = table_ref.shape[1]
    group = sent_ref.shape[3]
    columns = slot_columns(table_ref[...], patch)
    lanes = lax.broadcasted_iota(jnp.int32, (patch, patch + 2 * HW), 1)
    picks = [
        jnp.where(lanes == columns[:, j : j + 1], 1.0, 0.0).astype(BF) for j in range(1, stencil)
    ]
    picks = jnp.concatenate(picks, axis=0)
    for t in range(frames_here):
        rows = pl.ds(t * patch, patch)
        extended = jnp.concatenate([low_ref[t], frames_ref[t], high_ref[t]], axis=0)
        taken = mm(picks, extended).astype(BF)
        gathered_ref[rows, 0:width] = frames_ref[t]
        for j in range(1, stencil):
            gathered_ref[rows, j * width : (j + 1) * width] = taken[(j - 1) * patch : j * patch]
        pre = mm(gathered_ref[rows, :], w_ref[...])
        pre_ref[rows, :] = pre
        gate = jax.nn.sigmoid(pre)
        hidden = (frames_ref[t].astype(F32) + pre * gate).astype(BF)
        for i in range(patch // group):
            sent_ref[i, 0, t] = hidden[i * group : (i + 1) * group]
            sent_ref[i, 1, t] = cot_ref[t, i * group : (i + 1) * group]


def conv_forward(frames, cotangent, low, high, table, w_conv, parts):
    frames_here, patch, width = frames.shape
    rows = frames_here * patch
    return pl.pallas_call(
        conv_forward_kernel,
        out_shape=(
            jax.ShapeDtypeStruct((parts, 2, frames_here, patch // parts, width), BF),
            jax.ShapeDtypeStruct((rows, width), F32),
            jax.ShapeDtypeStruct((rows, w_conv.shape[0]), BF),
        ),
        name="conv_forward",
    )(frames, cotangent, low, high, table, w_conv)


def attention_kernel(came_ref, w_ref, back_ref, parts_ref):
    parts, _, frames_here, group, width = came_ref.shape
    frames_all = parts * frames_here
    rows_all = frames_all * group
    head_dim = width // HEADS
    scaling = head_dim ** (-0.5)
    half = 8
    rows = frames_all * half
    hidden = came_ref[:, 0].reshape(rows_all, width)
    grads = came_ref[:, 1].reshape(rows_all, width)

    def halves(values):
        cube = values.reshape(frames_all, group, width)
        return [cube[:, s : s + half].reshape(rows, width) for s in range(0, group, half)]

    query = halves(mm(hidden, w_ref[0]))
    key = halves(mm(hidden, w_ref[1]))
    value = halves(mm(hidden, w_ref[2]))
    grad_out = halves(mm_nt(grads, w_ref[3]))
    lane_head = lax.broadcasted_iota(jnp.int32, (rows, width), 1) // head_dim
    same = (
        lax.broadcasted_iota(jnp.int32, (rows, rows), 0) % half
        == lax.broadcasted_iota(jnp.int32, (rows, rows), 1) % half
    )
    same = jnp.where(same, 1.0, 0.0).astype(F32).reshape(1, frames_all, half, rows)

    def spread(values):
        return jnp.concatenate(
            [jnp.where(lane_head == h, values, 0.0).astype(BF) for h in range(HEADS)], axis=0
        )

    def collect(values):
        total = jnp.where(lane_head == 0, values[0:rows], 0.0)
        for h in range(1, HEADS):
            total = jnp.where(lane_head == h, values[h * rows : (h + 1) * rows], total)
        return total

    results = []
    for q32, k32, v32, g32 in zip(query, key, value, grad_out):
        q, g = q32.astype(BF), g32.astype(BF)
        k_heads, v_heads = spread(k32), spread(v32)
        shape4 = (HEADS, frames_all, half, rows)
        scores = mm_nt(k_heads, q).reshape(shape4) * scaling
        expo = jnp.exp(scores - jnp.max(scores, axis=1, keepdims=True))
        probs = expo * (same / jnp.sum(expo, axis=1, keepdims=True))
        probs_b = probs.reshape(-1, rows).astype(BF)
        grad_probs = mm_nt(v_heads, g).reshape(shape4)
        inner = jnp.sum(probs * grad_probs, axis=1, keepdims=True)
        grad_scores = (scaling * probs * (grad_probs - inner)).reshape(-1, rows).astype(BF)
        results.append(
            (
                mm_tn(probs_b, v_heads),
                mm_tn(grad_scores, k_heads),
                collect(mm(grad_scores, q)),
                collect(mm(probs_b, g)),
            )
        )

    def joined(index):
        pieces = [r[index].reshape(frames_all, half, width) for r in results]
        return jnp.concatenate(pieces, axis=1).reshape(rows_all, width).astype(BF)

    attended, grad_query, grad_key, grad_value = (joined(i) for i in range(4))
    back = (
        grads.astype(F32)
        + mm_nt(grad_query, w_ref[0])
        + mm_nt(grad_key, w_ref[1])
        + mm_nt(grad_value, w_ref[2])
    )
    back_ref[...] = back.astype(BF).reshape(back_ref.shape)
    parts_ref[0:width] = mm_tn(hidden, grad_query).astype(parts_ref.dtype)
    parts_ref[1 * width : 2 * width] = mm_tn(hidden, grad_key).astype(parts_ref.dtype)
    parts_ref[2 * width : 3 * width] = mm_tn(hidden, grad_value).astype(parts_ref.dtype)
    parts_ref[3 * width : 4 * width] = mm_tn(attended, grads).astype(parts_ref.dtype)


def attention(came, w_attn):
    parts, _, frames_here, group, width = came.shape
    return pl.pallas_call(
        attention_kernel,
        out_shape=(
            jax.ShapeDtypeStruct((parts, frames_here, group, width), BF),
            jax.ShapeDtypeStruct((4 * width, width), BF),
        ),
        name="attention",
    )(came, w_attn)


def conv_backward_kernel(
    back_ref,
    pre_ref,
    gathered_ref,
    table_ref,
    w_ref,
    attn_ref,
    local_ref,
    low_ref,
    high_ref,
    weights_ref,
):
    parts, frames_here, group, width = back_ref.shape
    patch = parts * group
    stencil = table_ref.shape[1]
    columns = slot_columns(table_ref[...], patch)
    lane = lax.broadcasted_iota(jnp.int32, (patch, patch), 1)
    square = jnp.full((patch, patch), -1.0, F32)
    for j in range(stencil):
        square = jnp.where(lane == j, columns[:, j : j + 1].astype(F32), square)
    square = square.T
    target = lax.broadcasted_iota(jnp.int32, (patch + 2 * HW, patch), 0).astype(F32)
    puts = jnp.concatenate(
        [jnp.where(target == square[j : j + 1], 1.0, 0.0).astype(BF) for j in range(stencil)],
        axis=1,
    )
    pre = pre_ref[...]
    gate = jax.nn.sigmoid(pre)
    slope = gate * (1.0 + pre * (1.0 - gate))
    backs, grads = [], []
    for t in range(frames_here):
        back = jnp.concatenate([back_ref[i, t] for i in range(parts)], axis=0).astype(F32)
        backs.append(back)
        grads.append((back * slope[t * patch : (t + 1) * patch]).astype(BF))
    for t in range(frames_here):
        spread = mm_nt(grads[t], w_ref[...]).astype(BF)
        stacked = jnp.concatenate(
            [spread[:, j * width : (j + 1) * width] for j in range(stencil)], axis=0
        )
        extended = mm(puts, stacked)
        low_ref[t] = extended[0:HW].astype(low_ref.dtype)
        high_ref[t] = extended[patch + HW :].astype(high_ref.dtype)
        local_ref[t] = backs[t] + extended[HW : HW + patch]
    grad_pre = jnp.concatenate(grads, axis=0)
    grad_w = mm_tn(gathered_ref[...], grad_pre).astype(BF)
    conv_rows = grad_w.shape[0] // parts
    attn_rows = attn_ref.shape[0] // parts
    for i in range(parts):
        weights_ref[i, 0:conv_rows] = grad_w[i * conv_rows : (i + 1) * conv_rows]
        weights_ref[i, conv_rows:] = attn_ref[i * attn_rows : (i + 1) * attn_rows]


def conv_backward(back, pre, gathered, table, w_conv, attn_parts):
    parts, frames_here, group, width = back.shape
    patch = parts * group
    weight_rows = (w_conv.shape[0] + attn_parts.shape[0]) // parts
    return pl.pallas_call(
        conv_backward_kernel,
        out_shape=(
            jax.ShapeDtypeStruct((frames_here, patch, width), F32),
            jax.ShapeDtypeStruct((frames_here, HW, width), BF),
            jax.ShapeDtypeStruct((frames_here, HW, width), BF),
            jax.ShapeDtypeStruct((parts, weight_rows, width), BF),
        ),
        name="conv_backward",
    )(back, pre, gathered, table, w_conv, attn_parts)


TILE = 16
LANES = 128


def first_sum_kernel(came_ref, tiles_ref):
    total = came_ref[0].astype(F32)
    for i in range(1, came_ref.shape[0]):
        total = total + came_ref[i].astype(F32)
    total = total.astype(BF)
    columns = total.shape[1] // LANES
    count = total.shape[0] // TILE * columns
    for n in range(count):
        row, lane = n // columns * TILE, n % columns * LANES
        tiles_ref[n] = total[row : row + TILE, lane : lane + LANES]
    rest = tiles_ref.shape[0] - count
    if rest:
        tiles_ref[count:] = jnp.zeros((rest, TILE, LANES), BF)


def first_sum(came, tiles):
    return pl.pallas_call(
        first_sum_kernel,
        out_shape=jax.ShapeDtypeStruct((tiles, TILE, LANES), BF),
        name="first_sum",
    )(came)


def second_sum_kernel(scaling, came_ref, copies_ref):
    total = (jnp.sum(came_ref[...].astype(F32), axis=0) * scaling).astype(BF)
    for i in range(copies_ref.shape[0]):
        copies_ref[i] = total


def second_sum(came, scaling):
    return pl.pallas_call(
        functools.partial(second_sum_kernel, scaling),
        out_shape=jax.ShapeDtypeStruct(came.shape, BF),
        name="second_sum",
    )(came)


def untile_kernel(tiles_ref, copies_ref):
    rows, width = copies_ref.shape[1:]
    columns = width // LANES
    for n in range(rows // TILE * columns):
        row, lane = n // columns * TILE, n % columns * LANES
        tile = tiles_ref[n]
        for i in range(copies_ref.shape[0]):
            copies_ref[i, row : row + TILE, lane : lane + LANES] = tile


def untile(tiles, shape):
    return pl.pallas_call(
        untile_kernel, out_shape=jax.ShapeDtypeStruct(shape, BF), name="untile"
    )(tiles)


def unpack_kernel(sums_ref, conv_ref, attn_ref):
    parts = sums_ref.shape[0]
    conv_rows = conv_ref.shape[0] // parts
    attn_rows = attn_ref.shape[0] // parts
    for i in range(parts):
        conv_ref[i * conv_rows : (i + 1) * conv_rows] = sums_ref[i, 0:conv_rows]
        attn_ref[i * attn_rows : (i + 1) * attn_rows] = sums_ref[i, conv_rows:]


def unpack(sums, conv_rows, attn_rows):
    width = sums.shape[2]
    return pl.pallas_call(
        unpack_kernel,
        out_shape=(
            jax.ShapeDtypeStruct((conv_rows, width), BF),
            jax.ShapeDtypeStruct((attn_rows, width), BF),
        ),
        name="unpack",
    )(sums)


def exchange(values, axis):
    return lax.all_to_all(values, axis, 0, 0, tiled=True)


def to_neighbours(upward, downward):
    count = lax.axis_size("vert")
    steps = [(i, i + 1) for i in range(count - 1)]
    from_below = lax.ppermute(upward, "vert", steps)
    from_above = lax.ppermute(downward, "vert", [(b, a) for a, b in steps])
    return from_below, from_above


def body(frames, cotangent, table, w_conv, w_attn):
    frames_here, patch, width = frames.shape
    parts = lax.axis_size("tm")
    patches = lax.axis_size("vert")
    low, high = to_neighbours(frames[:, patch - HW :], frames[:, :HW])
    sent, pre, gathered = conv_forward(frames, cotangent, low, high, table, w_conv, parts)
    back_time, attn_parts = attention(exchange(sent, "tm"), w_attn)
    back = exchange(back_time, "tm")
    local, rim_low, rim_high, weights = conv_backward(
        back, pre, gathered, table, w_conv, attn_parts
    )
    from_below, from_above = to_neighbours(rim_high, rim_low)
    arrived = jnp.concatenate([from_below, from_above], axis=1).astype(F32)
    grad_frames = (local + arrived).astype(BF)
    count = weights[0].size // (TILE * LANES)
    each = -(-count // patches)
    tiles = first_sum(exchange(weights, "tm"), each * patches)
    scaling = 1.0 / math.sqrt(TF * patch * patches)
    came = exchange(tiles, "vert").reshape(patches, each, TILE, LANES)
    copies = second_sum(came, scaling).reshape(tiles.shape)
    copies = untile(exchange(copies, "vert"), weights.shape)
    grad_conv, grad_attn = unpack(exchange(copies, "tm"), w_conv.shape[0], attn_parts.shape[0])
    return grad_frames, grad_conv, grad_attn.reshape(w_attn.shape)


def solution(mesh):
    return jax.shard_map(
        body,
        mesh=mesh,
        in_specs=(P("tm", "vert", None), P("tm", "vert", None), P("vert", None), P(), P()),
        out_specs=(P("tm", "vert", None), P(), P()),
        check_vma=False,
    )
```

```python
import functools
import math

import jax
import jax.numpy as jnp
from jax import lax
from jax.experimental import pallas as pl
from jax.experimental.pallas import tpu as pltpu
from jax.sharding import PartitionSpec as P

TF = 16
HEADS = 8
HW = 64
TM = ("x", "z_hi")
VERT = ("y", "z_lo", "core")
NEAR = ("x", "core")
FAR = ("z_hi", "y", "z_lo")
BF = jnp.bfloat16
F32 = jnp.float32


def mm(left, right):
    return jnp.dot(left, right, preferred_element_type=F32)


def mm_nt(left, right):
    return lax.dot_general(left, right, (((1,), (1,)), ((), ())), preferred_element_type=F32)


def mm_tn(left, right):
    return lax.dot_general(left, right, (((0,), (0,)), ((), ())), preferred_element_type=F32)


def slot_places(table):
    lanes = lax.broadcasted_iota(jnp.int32, table.shape, 1)
    return jnp.where(table < 0, -1, table - table[0:1] + lanes + HW).astype(F32)


def conv_forward_kernel(
    frames_ref, cot_ref, low_ref, high_ref, table_ref, w_ref, sent_ref, pre_ref, gathered_ref
):
    frames_here, patch, width = frames_ref.shape
    stencil = table_ref.shape[0]
    group = sent_ref.shape[3]
    places = slot_places(table_ref[...])
    row = lax.broadcasted_iota(jnp.int32, (patch, patch), 0)
    square = jnp.full((patch, patch), -1.0, F32)
    for j in range(1, stencil):
        square = jnp.where(row == j, places[j : j + 1], square)
    columns = square.T
    lanes = lax.broadcasted_iota(jnp.int32, (patch, patch + 2 * HW), 1).astype(F32)
    picks = [
        jnp.where(lanes == columns[:, j : j + 1], 1.0, 0.0).astype(BF) for j in range(1, stencil)
    ]
    picks = jnp.concatenate(picks, axis=0)
    for t in range(frames_here):
        rows = pl.ds(t * patch, patch)
        extended = jnp.concatenate([low_ref[t], frames_ref[t], high_ref[t]], axis=0)
        taken = mm(picks, extended).astype(BF)
        gathered_ref[rows, 0:width] = frames_ref[t]
        for j in range(1, stencil):
            gathered_ref[rows, j * width : (j + 1) * width] = taken[(j - 1) * patch : j * patch]
        pre = mm(gathered_ref[rows, :], w_ref[...])
        pre_ref[rows, :] = pre
        gate = jax.nn.sigmoid(pre)
        hidden = (frames_ref[t].astype(F32) + pre * gate).astype(BF)
        for i in range(patch // group):
            sent_ref[i, 0, t] = hidden[i * group : (i + 1) * group]
            sent_ref[i, 1, t] = cot_ref[t, i * group : (i + 1) * group]


def conv_forward(frames, cotangent, low, high, table, w_conv, parts):
    frames_here, patch, width = frames.shape
    rows = frames_here * patch
    return pl.pallas_call(
        conv_forward_kernel,
        out_shape=(
            jax.ShapeDtypeStruct((parts, 2, frames_here, patch // parts, width), BF),
            jax.ShapeDtypeStruct((rows, width), F32),
            jax.ShapeDtypeStruct((rows, w_conv.shape[0]), BF),
        ),
        name="conv_forward",
    )(frames, cotangent, low, high, table, w_conv)


def attention_kernel(came_ref, w_ref, back_ref, parts_ref):
    parts, _, frames_here, group, width = came_ref.shape
    frames_all = parts * frames_here
    rows_all = frames_all * group
    head_dim = width // HEADS
    scaling = head_dim ** (-0.5)
    half = 8
    rows = frames_all * half
    hidden = came_ref[:, 0].reshape(rows_all, width)
    grads = came_ref[:, 1].reshape(rows_all, width)

    def halves(values):
        cube = values.reshape(frames_all, group, width)
        return [cube[:, s : s + half].reshape(rows, width) for s in range(0, group, half)]

    query = halves(mm(hidden, w_ref[0]))
    key = halves(mm(hidden, w_ref[1]))
    value = halves(mm(hidden, w_ref[2]))
    grad_out = halves(mm_nt(grads, w_ref[3]))
    lane_head = lax.broadcasted_iota(jnp.int32, (rows, width), 1) // head_dim
    same = (
        lax.broadcasted_iota(jnp.int32, (rows, rows), 0) % half
        == lax.broadcasted_iota(jnp.int32, (rows, rows), 1) % half
    )
    same = jnp.where(same, 1.0, 0.0).astype(F32).reshape(1, frames_all, half, rows)

    def spread(values):
        return jnp.concatenate(
            [jnp.where(lane_head == h, values, 0.0).astype(BF) for h in range(HEADS)], axis=0
        )

    def collect(values):
        total = jnp.where(lane_head == 0, values[0:rows], 0.0)
        for h in range(1, HEADS):
            total = jnp.where(lane_head == h, values[h * rows : (h + 1) * rows], total)
        return total

    results = []
    for q32, k32, v32, g32 in zip(query, key, value, grad_out):
        q, g = q32.astype(BF), g32.astype(BF)
        k_heads, v_heads = spread(k32), spread(v32)
        shape4 = (HEADS, frames_all, half, rows)
        scores = mm_nt(k_heads, q).reshape(shape4) * scaling
        expo = jnp.exp(scores - jnp.max(scores, axis=1, keepdims=True))
        probs = expo * (same / jnp.sum(expo, axis=1, keepdims=True))
        probs_b = probs.reshape(-1, rows).astype(BF)
        grad_probs = mm_nt(v_heads, g).reshape(shape4)
        inner = jnp.sum(probs * grad_probs, axis=1, keepdims=True)
        grad_scores = (scaling * probs * (grad_probs - inner)).reshape(-1, rows).astype(BF)
        results.append(
            (
                mm_tn(probs_b, v_heads),
                mm_tn(grad_scores, k_heads),
                collect(mm(grad_scores, q)),
                collect(mm(probs_b, g)),
            )
        )

    def joined(index):
        pieces = [r[index].reshape(frames_all, half, width) for r in results]
        return jnp.concatenate(pieces, axis=1).reshape(rows_all, width).astype(BF)

    attended, grad_query, grad_key, grad_value = (joined(i) for i in range(4))
    back = (
        grads.astype(F32)
        + mm_nt(grad_query, w_ref[0])
        + mm_nt(grad_key, w_ref[1])
        + mm_nt(grad_value, w_ref[2])
    )
    back_ref[...] = back.astype(BF).reshape(back_ref.shape)
    parts_ref[0:width] = mm_tn(hidden, grad_query).astype(parts_ref.dtype)
    parts_ref[1 * width : 2 * width] = mm_tn(hidden, grad_key).astype(parts_ref.dtype)
    parts_ref[2 * width : 3 * width] = mm_tn(hidden, grad_value).astype(parts_ref.dtype)
    parts_ref[3 * width : 4 * width] = mm_tn(attended, grads).astype(parts_ref.dtype)


def attention(came, w_attn):
    parts, _, frames_here, group, width = came.shape
    return pl.pallas_call(
        attention_kernel,
        out_shape=(
            jax.ShapeDtypeStruct((parts, frames_here, group, width), BF),
            jax.ShapeDtypeStruct((4 * width, width), BF),
        ),
        name="attention",
    )(came, w_attn)


def conv_backward_kernel(
    back_ref,
    pre_ref,
    gathered_ref,
    table_ref,
    w_ref,
    attn_ref,
    local_ref,
    low_ref,
    high_ref,
    weights_ref,
):
    parts, frames_here, group, width = back_ref.shape
    patch = parts * group
    stencil = table_ref.shape[0]
    places = slot_places(table_ref[...])
    target = lax.broadcasted_iota(jnp.int32, (patch + 2 * HW, patch), 0).astype(F32)
    puts = jnp.concatenate(
        [jnp.where(target == places[j : j + 1], 1.0, 0.0).astype(BF) for j in range(stencil)],
        axis=1,
    )
    pre = pre_ref[...]
    gate = jax.nn.sigmoid(pre)
    slope = gate * (1.0 + pre * (1.0 - gate))
    backs, grads = [], []
    for t in range(frames_here):
        back = jnp.concatenate([back_ref[i, t] for i in range(parts)], axis=0).astype(F32)
        backs.append(back)
        grads.append((back * slope[t * patch : (t + 1) * patch]).astype(BF))
    for t in range(frames_here):
        spread = mm_nt(grads[t], w_ref[...]).astype(BF)
        stacked = jnp.concatenate(
            [spread[:, j * width : (j + 1) * width] for j in range(stencil)], axis=0
        )
        extended = mm(puts, stacked)
        low_ref[t] = extended[0:HW].astype(low_ref.dtype)
        high_ref[t] = extended[patch + HW :].astype(high_ref.dtype)
        local_ref[t] = backs[t] + extended[HW : HW + patch]
    grad_pre = jnp.concatenate(grads, axis=0)
    grad_w = mm_tn(gathered_ref[...], grad_pre).astype(BF)
    near = weights_ref.shape[0]
    conv_rows = grad_w.shape[0] // near
    attn_rows = attn_ref.shape[0] // near
    for i in range(near):
        weights_ref[i, 0:conv_rows] = grad_w[i * conv_rows : (i + 1) * conv_rows]
        weights_ref[i, conv_rows:] = attn_ref[i * attn_rows : (i + 1) * attn_rows]


def conv_backward(back, pre, gathered, table, w_conv, attn_parts, near):
    parts, frames_here, group, width = back.shape
    patch = parts * group
    weight_rows = (w_conv.shape[0] + attn_parts.shape[0]) // near
    return pl.pallas_call(
        conv_backward_kernel,
        out_shape=(
            jax.ShapeDtypeStruct((frames_here, patch, width), F32),
            jax.ShapeDtypeStruct((frames_here, HW, width), BF),
            jax.ShapeDtypeStruct((frames_here, HW, width), BF),
            jax.ShapeDtypeStruct((near, weight_rows, width), BF),
        ),
        name="conv_backward",
    )(back, pre, gathered, table, w_conv, attn_parts)


TILE = 16
LANES = 128


def first_sum_kernel(came_ref, tiles_ref):
    total = came_ref[0].astype(F32)
    for i in range(1, came_ref.shape[0]):
        total = total + came_ref[i].astype(F32)
    total = total.astype(BF)
    columns = total.shape[1] // LANES
    count = total.shape[0] // TILE * columns
    for n in range(count):
        row, lane = n // columns * TILE, n % columns * LANES
        tiles_ref[n] = total[row : row + TILE, lane : lane + LANES]
    rest = tiles_ref.shape[0] - count
    if rest:
        tiles_ref[count:] = jnp.zeros((rest, TILE, LANES), BF)


def first_sum(came, tiles):
    return pl.pallas_call(
        first_sum_kernel,
        out_shape=jax.ShapeDtypeStruct((tiles, TILE, LANES), BF),
        name="first_sum",
    )(came)


def second_sum_kernel(scaling, came_ref, copies_ref):
    total = (jnp.sum(came_ref[...].astype(F32), axis=0) * scaling).astype(BF)
    for i in range(copies_ref.shape[0]):
        copies_ref[i] = total


def second_sum(came, scaling):
    return pl.pallas_call(
        functools.partial(second_sum_kernel, scaling),
        out_shape=jax.ShapeDtypeStruct(came.shape, BF),
        name="second_sum",
    )(came)


def untile_kernel(tiles_ref, copies_ref, whole_ref, sem):
    rows, width = whole_ref.shape
    columns = width // LANES
    for n in range(rows // TILE * columns):
        row, lane = n // columns * TILE, n % columns * LANES
        whole_ref[row : row + TILE, lane : lane + LANES] = tiles_ref[n]
    count = copies_ref.shape[0]
    moves = [pltpu.make_async_copy(whole_ref, copies_ref.at[i], sem.at[i]) for i in range(count)]
    for move in moves:
        move.start()
    for move in moves:
        move.wait()


def untile(tiles, shape):
    return pl.pallas_call(
        untile_kernel,
        out_shape=jax.ShapeDtypeStruct(shape, BF),
        out_specs=pl.BlockSpec(memory_space=pl.ANY),
        scratch_shapes=[pltpu.VMEM(shape[1:], BF), pltpu.SemaphoreType.DMA((shape[0],))],
        name="untile",
    )(tiles)


def unpack_kernel(sums_ref, conv_ref, attn_ref, sem):
    conv_rows = conv_ref.shape[1]
    attn_rows = attn_ref.shape[1]
    moves = []
    for i in range(sums_ref.shape[0]):
        moves.append(
            pltpu.make_async_copy(sums_ref.at[i, 0:conv_rows], conv_ref.at[i], sem.at[0, i])
        )
        moves.append(
            pltpu.make_async_copy(
                sums_ref.at[i, conv_rows : conv_rows + attn_rows], attn_ref.at[i], sem.at[1, i]
            )
        )
    for move in moves:
        move.start()
    for move in moves:
        move.wait()


def unpack(sums, conv_rows, attn_rows):
    near, _, width = sums.shape
    return pl.pallas_call(
        unpack_kernel,
        out_shape=(
            jax.ShapeDtypeStruct((near, conv_rows // near, width), BF),
            jax.ShapeDtypeStruct((near, attn_rows // near, width), BF),
        ),
        in_specs=[pl.BlockSpec(memory_space=pl.ANY)],
        out_specs=[pl.BlockSpec(memory_space=pl.ANY)] * 2,
        scratch_shapes=[pltpu.SemaphoreType.DMA((2, near))],
        name="unpack",
    )(sums)


def exchange(values, axis):
    return lax.all_to_all(values, axis, 0, 0, tiled=True)


def to_neighbours(upward, downward):
    count = lax.axis_size(VERT)
    steps = [(i, i + 1) for i in range(count - 1)]
    from_below = lax.ppermute(upward, VERT, steps)
    from_above = lax.ppermute(downward, VERT, [(b, a) for a, b in steps])
    return from_below, from_above


def body(frames, cotangent, table, w_conv, w_attn):
    frames_here, patch, width = frames.shape
    parts = lax.axis_size(TM)
    patches = lax.axis_size(VERT)
    low, high = to_neighbours(frames[:, patch - HW :], frames[:, :HW])
    sent, pre, gathered = conv_forward(frames, cotangent, low, high, table.T, w_conv, parts)
    back_time, attn_parts = attention(exchange(sent, TM), w_attn)
    back = exchange(back_time, TM)
    local, rim_low, rim_high, weights = conv_backward(
        back, pre, gathered, table.T, w_conv, attn_parts, lax.axis_size(NEAR)
    )
    from_below, from_above = to_neighbours(rim_high, rim_low)
    arrived = jnp.concatenate([from_below, from_above], axis=1).astype(F32)
    grad_frames = (local + arrived).astype(BF)
    far = lax.axis_size(FAR)
    count = weights[0].size // (TILE * LANES)
    each = -(-count // far)
    tiles = first_sum(exchange(weights, NEAR), each * far)
    scaling = 1.0 / math.sqrt(TF * patch * patches)
    came = exchange(tiles, FAR).reshape(far, each, TILE, LANES)
    copies = second_sum(came, scaling).reshape(tiles.shape)
    copies = untile(exchange(copies, FAR), weights.shape)
    grad_conv, grad_attn = unpack(exchange(copies, NEAR), w_conv.shape[0], attn_parts.shape[0])
    return grad_frames, grad_conv.reshape(w_conv.shape), grad_attn.reshape(w_attn.shape)


def solution(mesh):
    parts, patches = mesh.devices.shape
    sizes = (parts // 2, 2, patches // 8, 4, 2)
    fine = jax.sharding.Mesh(mesh.devices.reshape(sizes), TM + VERT)
    return jax.shard_map(
        body,
        mesh=fine,
        in_specs=(P(TM, VERT, None), P(TM, VERT, None), P(VERT, None), P(), P()),
        out_specs=(P(TM, VERT, None), P(), P()),
        check_vma=False,
    )
```

```python
import functools
import math

import jax
import jax.numpy as jnp
from jax import lax
from jax.experimental import pallas as pl
from jax.experimental.pallas import tpu as pltpu
from jax.sharding import PartitionSpec as P

TF = 16
HEADS = 8
HW = 64
TM = ("x_hi", "x_lo", "z_hi")
VERT = ("y_hi", "y_lo", "z_mid", "z_lo", "core")
NEAR = ("x_lo", "y_lo", "z_lo", "core")
FAR = ("x_hi", "z_hi", "y_hi", "z_mid")
TILE = 16
BF = jnp.bfloat16
F32 = jnp.float32

LIMIT = pltpu.CompilerParams(vmem_limit_bytes=32 * 1024 * 1024)


def mm(left, right):
    return jnp.dot(left, right, preferred_element_type=F32)


def mm_nt(left, right):
    return lax.dot_general(left, right, (((1,), (1,)), ((), ())), preferred_element_type=F32)


def mm_tn(left, right):
    return lax.dot_general(left, right, (((0,), (0,)), ((), ())), preferred_element_type=F32)


def slot_places(table):
    lanes = lax.broadcasted_iota(jnp.int32, table.shape, 1)
    return jnp.where(table < 0, -1, table - table[0:1] + lanes + HW).astype(F32)


def conv_forward_kernel(
    frames_ref, cot_ref, low_ref, high_ref, table_ref, w_ref, sent_ref, pre_ref, gathered_ref
):
    frames_here, patch, width = frames_ref.shape
    stencil = table_ref.shape[0]
    group = sent_ref.shape[3]
    places = slot_places(table_ref[...])
    row = lax.broadcasted_iota(jnp.int32, (patch, patch), 0)
    square = jnp.full((patch, patch), -1.0, F32)
    for j in range(1, stencil):
        square = jnp.where(row == j, places[j : j + 1], square)
    columns = square.T
    lanes = lax.broadcasted_iota(jnp.int32, (patch, patch + 2 * HW), 1).astype(F32)
    picks = [
        jnp.where(lanes == columns[:, j : j + 1], 1.0, 0.0).astype(BF) for j in range(1, stencil)
    ]
    picks = jnp.concatenate(picks, axis=0)
    for t in range(frames_here):
        rows = pl.ds(t * patch, patch)
        extended = jnp.concatenate([low_ref[t], frames_ref[t], high_ref[t]], axis=0)
        taken = mm(picks, extended).astype(BF)
        gathered_ref[rows, 0:width] = frames_ref[t]
        for j in range(1, stencil):
            gathered_ref[rows, j * width : (j + 1) * width] = taken[(j - 1) * patch : j * patch]
        pre = mm(gathered_ref[rows, :], w_ref[...])
        pre_ref[rows, :] = pre
        gate = jax.nn.sigmoid(pre)
        hidden = (frames_ref[t].astype(F32) + pre * gate).astype(BF)
        for i in range(patch // group):
            sent_ref[i, 0, t] = hidden[i * group : (i + 1) * group]
            sent_ref[i, 1, t] = cot_ref[t, i * group : (i + 1) * group]


def conv_forward(frames, cotangent, low, high, table, w_conv, parts):
    frames_here, patch, width = frames.shape
    rows = frames_here * patch
    return pl.pallas_call(
        conv_forward_kernel,
        out_shape=(
            pltpu.VMEM((parts, 2, frames_here, patch // parts, width), BF),
            pltpu.VMEM((rows, width), F32),
            pltpu.VMEM((rows, w_conv.shape[0]), BF),
        ),
        name="conv_forward",
        compiler_params=LIMIT,
    )(frames, cotangent, here(low), here(high), table, w_conv)


def attention_kernel(came_ref, w_ref, back_ref, parts_ref):
    parts, _, frames_here, group, width = came_ref.shape
    frames_all = parts * frames_here
    rows_all = frames_all * group
    head_dim = width // HEADS
    scaling = head_dim ** (-0.5)
    half = 8
    rows = frames_all * half
    hidden = came_ref[:, 0].reshape(rows_all, width)
    grads = came_ref[:, 1].reshape(rows_all, width)

    def halves(values):
        cube = values.reshape(frames_all, group, width)
        return [cube[:, s : s + half].reshape(rows, width) for s in range(0, group, half)]

    query = halves(mm(hidden, w_ref[0]))
    key = halves(mm(hidden, w_ref[1]))
    value = halves(mm(hidden, w_ref[2]))
    grad_out = halves(mm_nt(grads, w_ref[3]))
    lane_head = lax.broadcasted_iota(jnp.int32, (rows, width), 1) // head_dim
    same = (
        lax.broadcasted_iota(jnp.int32, (rows, rows), 0) % half
        == lax.broadcasted_iota(jnp.int32, (rows, rows), 1) % half
    )
    same = jnp.where(same, 1.0, 0.0).astype(F32).reshape(1, frames_all, half, rows)

    def spread(values):
        return jnp.concatenate(
            [jnp.where(lane_head == h, values, 0.0).astype(BF) for h in range(HEADS)], axis=0
        )

    def collect(values):
        total = jnp.where(lane_head == 0, values[0:rows], 0.0)
        for h in range(1, HEADS):
            total = jnp.where(lane_head == h, values[h * rows : (h + 1) * rows], total)
        return total

    results = []
    for q32, k32, v32, g32 in zip(query, key, value, grad_out):
        q, g = q32.astype(BF), g32.astype(BF)
        k_heads, v_heads = spread(k32), spread(v32)
        shape4 = (HEADS, frames_all, half, rows)
        scores = mm_nt(k_heads, q).reshape(shape4) * scaling
        expo = jnp.exp(scores - jnp.max(scores, axis=1, keepdims=True))
        probs = expo * (same / jnp.sum(expo, axis=1, keepdims=True))
        probs_b = probs.reshape(-1, rows).astype(BF)
        grad_probs = mm_nt(v_heads, g).reshape(shape4)
        inner = jnp.sum(probs * grad_probs, axis=1, keepdims=True)
        grad_scores = (scaling * probs * (grad_probs - inner)).reshape(-1, rows).astype(BF)
        results.append(
            (
                mm_tn(probs_b, v_heads),
                mm_tn(grad_scores, k_heads),
                collect(mm(grad_scores, q)),
                collect(mm(probs_b, g)),
            )
        )

    def joined(index):
        pieces = [r[index].reshape(frames_all, half, width) for r in results]
        return jnp.concatenate(pieces, axis=1).reshape(rows_all, width).astype(BF)

    attended, grad_query, grad_key, grad_value = (joined(i) for i in range(4))
    back = (
        grads.astype(F32)
        + mm_nt(grad_query, w_ref[0])
        + mm_nt(grad_key, w_ref[1])
        + mm_nt(grad_value, w_ref[2])
    )
    back_ref[...] = back.astype(BF).reshape(back_ref.shape)
    parts_ref[0:width] = mm_tn(hidden, grad_query).astype(parts_ref.dtype)
    parts_ref[1 * width : 2 * width] = mm_tn(hidden, grad_key).astype(parts_ref.dtype)
    parts_ref[2 * width : 3 * width] = mm_tn(hidden, grad_value).astype(parts_ref.dtype)
    parts_ref[3 * width : 4 * width] = mm_tn(attended, grads).astype(parts_ref.dtype)


def attention(came, w_attn):
    parts, _, frames_here, group, width = came.shape
    return pl.pallas_call(
        attention_kernel,
        out_shape=(
            pltpu.VMEM((parts, frames_here, group, width), BF),
            pltpu.VMEM((4 * width, width), BF),
        ),
        name="attention",
        compiler_params=LIMIT,
    )(here(came), w_attn)


def conv_backward_kernel(
    back_ref,
    pre_ref,
    gathered_ref,
    table_ref,
    w_ref,
    attn_ref,
    local_ref,
    low_ref,
    high_ref,
    weights_ref,
):
    parts, frames_here, group, width = back_ref.shape
    patch = parts * group
    stencil = table_ref.shape[0]
    places = slot_places(table_ref[...])
    target = lax.broadcasted_iota(jnp.int32, (patch + 2 * HW, patch), 0).astype(F32)
    puts = jnp.concatenate(
        [jnp.where(target == places[j : j + 1], 1.0, 0.0).astype(BF) for j in range(stencil)],
        axis=1,
    )
    pre = pre_ref[...]
    gate = jax.nn.sigmoid(pre)
    slope = gate * (1.0 + pre * (1.0 - gate))
    backs, grads = [], []
    for t in range(frames_here):
        back = jnp.concatenate([back_ref[i, t] for i in range(parts)], axis=0).astype(F32)
        backs.append(back)
        grads.append((back * slope[t * patch : (t + 1) * patch]).astype(BF))
    for t in range(frames_here):
        spread = mm_nt(grads[t], w_ref[...]).astype(BF)
        stacked = jnp.concatenate(
            [spread[:, j * width : (j + 1) * width] for j in range(stencil)], axis=0
        )
        extended = mm(puts, stacked)
        low_ref[t] = extended[0:HW].astype(low_ref.dtype)
        high_ref[t] = extended[patch + HW :].astype(high_ref.dtype)
        local_ref[t] = backs[t] + extended[HW : HW + patch]
    grad_pre = jnp.concatenate(grads, axis=0)
    grad_w = mm_tn(gathered_ref[...], grad_pre).astype(BF)
    near = weights_ref.shape[0]
    conv_rows = grad_w.shape[0] // near
    attn_rows = attn_ref.shape[0] // near
    for i in range(near):
        weights_ref[i, 0:conv_rows] = grad_w[i * conv_rows : (i + 1) * conv_rows]
        weights_ref[i, conv_rows:] = attn_ref[i * attn_rows : (i + 1) * attn_rows]


def conv_backward(back, pre, gathered, table, w_conv, attn_parts, near):
    parts, frames_here, group, width = back.shape
    patch = parts * group
    weight_rows = (w_conv.shape[0] + attn_parts.shape[0]) // near
    return pl.pallas_call(
        conv_backward_kernel,
        out_shape=(
            pltpu.VMEM((frames_here, patch, width), F32),
            pltpu.VMEM((frames_here, HW, width), BF),
            pltpu.VMEM((frames_here, HW, width), BF),
            pltpu.VMEM((near, weight_rows, width), BF),
        ),
        name="conv_backward",
        compiler_params=LIMIT,
    )(here(back), here(pre), here(gathered), table, w_conv, here(attn_parts))


LANES = 128


def first_sum_kernel(came_ref, tiles_ref):
    total = came_ref[0].astype(F32)
    for i in range(1, came_ref.shape[0]):
        total = total + came_ref[i].astype(F32)
    total = total.astype(BF)
    columns = total.shape[1] // LANES
    count = total.shape[0] // TILE * columns
    for n in range(count):
        row, lane = n // columns * TILE, n % columns * LANES
        tiles_ref[n] = total[row : row + TILE, lane : lane + LANES]
    rest = tiles_ref.shape[0] - count
    if rest:
        tiles_ref[count:] = jnp.zeros((rest, TILE, LANES), BF)


def first_sum(came, tiles):
    return pl.pallas_call(
        first_sum_kernel,
        out_shape=pltpu.VMEM((tiles, TILE, LANES), BF),
        name="first_sum",
        compiler_params=LIMIT,
    )(here(came))


def second_sum_kernel(scaling, came_ref, copies_ref):
    total = (jnp.sum(came_ref[...].astype(F32), axis=0) * scaling).astype(BF)
    for i in range(copies_ref.shape[0]):
        copies_ref[i] = total


def second_sum(came, scaling):
    return pl.pallas_call(
        functools.partial(second_sum_kernel, scaling),
        out_shape=pltpu.VMEM(came.shape, BF),
        name="second_sum",
        compiler_params=LIMIT,
    )(here(came))


def untile_kernel(tiles_ref, copies_ref):
    rows, width = copies_ref.shape[1:]
    columns = width // LANES
    for n in range(rows // TILE * columns):
        row, lane = n // columns * TILE, n % columns * LANES
        tile = tiles_ref[n]
        for i in range(copies_ref.shape[0]):
            copies_ref[i, row : row + TILE, lane : lane + LANES] = tile


def untile(tiles, shape):
    return pl.pallas_call(
        untile_kernel, out_shape=pltpu.VMEM(shape, BF), name="untile", compiler_params=LIMIT
    )(here(tiles))


def unpack_kernel(sums_ref, conv_ref, attn_ref, sem):
    conv_rows = conv_ref.shape[1]
    moves = [
        pltpu.make_async_copy(sums_ref.at[:, 0:conv_rows], conv_ref, sem.at[0]),
        pltpu.make_async_copy(sums_ref.at[:, conv_rows:], attn_ref, sem.at[1]),
    ]
    for move in moves:
        move.start()
    for move in moves:
        move.wait()


def unpack(sums, conv_rows, attn_rows):
    near, _, width = sums.shape
    return pl.pallas_call(
        unpack_kernel,
        out_shape=(
            jax.ShapeDtypeStruct((near, conv_rows // near, width), BF),
            jax.ShapeDtypeStruct((near, attn_rows // near, width), BF),
        ),
        in_specs=[pl.BlockSpec(memory_space=pltpu.VMEM)],
        out_specs=[pl.BlockSpec(memory_space=pl.ANY)] * 2,
        scratch_shapes=[pltpu.SemaphoreType.DMA((2,))],
        name="unpack",
        compiler_params=LIMIT,
    )(here(sums))


def exchange(values, axis):
    return lax.all_to_all(values, axis, 0, 0, tiled=True)


def here(values):
    return pltpu.with_memory_space_constraint(values, pltpu.VMEM)


def to_neighbours(upward, downward):
    count = lax.axis_size(VERT)
    steps = [(i, i + 1) for i in range(count - 1)]
    from_below = lax.ppermute(upward, VERT, steps)
    from_above = lax.ppermute(downward, VERT, [(b, a) for a, b in steps])
    return from_below, from_above


def body(frames, cotangent, table, w_conv, w_attn):
    frames_here, patch, width = frames.shape
    parts = lax.axis_size(TM)
    patches = lax.axis_size(VERT)
    low, high = to_neighbours(frames[:, patch - HW :], frames[:, :HW])
    sent, pre, gathered = conv_forward(frames, cotangent, low, high, table.T, w_conv, parts)
    back_time, attn_parts = attention(exchange(sent, TM), w_attn)
    back = exchange(back_time, TM)
    local, rim_low, rim_high, weights = conv_backward(
        back, pre, gathered, table.T, w_conv, attn_parts, lax.axis_size(NEAR)
    )
    from_below, from_above = to_neighbours(rim_high, rim_low)
    arrived = jnp.concatenate([from_below, from_above], axis=1).astype(F32)
    grad_frames = (local + arrived).astype(BF)
    far = lax.axis_size(FAR)
    count = weights[0].size // (TILE * LANES)
    each = -(-count // far)
    tiles = first_sum(exchange(weights, NEAR), each * far)
    scaling = 1.0 / math.sqrt(TF * patch * patches)
    came = exchange(tiles, FAR).reshape(far, each, TILE, LANES)
    copies = second_sum(came, scaling).reshape(tiles.shape)
    copies = untile(exchange(copies, FAR), weights.shape)
    grad_conv, grad_attn = unpack(exchange(copies, NEAR), w_conv.shape[0], attn_parts.shape[0])
    return grad_frames, grad_conv.reshape(w_conv.shape), grad_attn.reshape(w_attn.shape)


def solution(mesh):
    parts, patches = mesh.devices.shape
    sizes = (parts // 4, 2, 2, patches // 16, 2, 2, 2, 2)
    fine = jax.sharding.Mesh(mesh.devices.reshape(sizes), TM + VERT)
    return jax.shard_map(
        body,
        mesh=fine,
        in_specs=(P(TM, VERT, None), P(TM, VERT, None), P(VERT, None), P(), P()),
        out_specs=(P(TM, VERT, None), P(), P()),
        check_vma=False,
    )
```

```python
import functools
import math

import jax
import jax.numpy as jnp
from jax import lax
from jax.experimental import pallas as pl
from jax.experimental.pallas import tpu as pltpu
from jax.sharding import PartitionSpec as P


TF = 16
HEADS = 8
HW = 64
TM = ("x_hi", "x_lo", "z_hi")
VERT = ("y_hi", "y_lo", "z_mid", "z_lo", "core")
PAIR = "core"
NEAR = ("x_lo", "y_lo", "z_lo")
FAR = ("x_hi", "z_hi", "y_hi", "z_mid")
TILE = 16
BF = jnp.bfloat16
F32 = jnp.float32

LIMIT = pltpu.CompilerParams(vmem_limit_bytes=32 * 1024 * 1024)


def mm(left, right):
    return jnp.dot(left, right, preferred_element_type=F32)


def mm_nt(left, right):
    return lax.dot_general(left, right, (((1,), (1,)), ((), ())), preferred_element_type=F32)


def mm_tn(left, right):
    return lax.dot_general(left, right, (((0,), (0,)), ((), ())), preferred_element_type=F32)


def slot_places(table):
    lanes = lax.broadcasted_iota(jnp.int32, table.shape, 1)
    return jnp.where(table < 0, -1, table - table[0:1] + lanes + HW).astype(F32)


def stage_kernel(
    frames_ref, cot_ref, table_ref, w_ref, frames_out, cot_out, table_out, w_out, picks_ref, sem
):
    pairs = (
        (table_ref, table_out),
        (w_ref, w_out),
        (frames_ref, frames_out),
        (cot_ref, cot_out),
    )
    moves = [pltpu.make_async_copy(a, b, sem.at[i]) for i, (a, b) in enumerate(pairs)]
    for move in moves:
        move.start()
    moves[0].wait()
    stencil, patch = table_out.shape
    places = slot_places(table_out[...])
    row = lax.broadcasted_iota(jnp.int32, (patch, patch), 0)
    square = jnp.full((patch, patch), -1.0, F32)
    for j in range(1, stencil):
        square = jnp.where(row == j, places[j : j + 1], square)
    columns = square.T
    lanes = lax.broadcasted_iota(jnp.int32, (patch, patch + 2 * HW), 1).astype(F32)
    for j in range(1, stencil):
        picks_ref[(j - 1) * patch : j * patch, :] = jnp.where(
            lanes == columns[:, j : j + 1], 1.0, 0.0
        ).astype(BF)
    for move in moves[1:]:
        move.wait()


def stage(frames, cotangent, table, w_conv):
    stencil, patch = table.shape
    return pl.pallas_call(
        stage_kernel,
        out_shape=(
            pltpu.VMEM(frames.shape, BF),
            pltpu.VMEM(cotangent.shape, BF),
            pltpu.VMEM(table.shape, jnp.int32),
            pltpu.VMEM(w_conv.shape, BF),
            pltpu.VMEM(((stencil - 1) * patch, patch + 2 * HW), BF),
        ),
        in_specs=[pl.BlockSpec(memory_space=pl.ANY)] * 4,
        scratch_shapes=[pltpu.SemaphoreType.DMA((4,))],
        name="stage",
        compiler_params=LIMIT,
    )(*(far_off(x) for x in (frames, cotangent, table, w_conv)))


def conv_forward_kernel(
    frames_ref, cot_ref, low_ref, high_ref, picks_ref, w_ref, sent_ref, pre_ref, gathered_ref
):
    frames_here, patch, width = frames_ref.shape
    stencil = picks_ref.shape[0] // patch + 1
    group = sent_ref.shape[3]
    for t in range(frames_here):
        rows = pl.ds(t * patch, patch)
        extended = jnp.concatenate([low_ref[t], frames_ref[t], high_ref[t]], axis=0)
        taken = mm(picks_ref[...], extended).astype(BF)
        gathered_ref[rows, 0:width] = frames_ref[t]
        for j in range(1, stencil):
            gathered_ref[rows, j * width : (j + 1) * width] = taken[(j - 1) * patch : j * patch]
        pre = mm(gathered_ref[rows, :], w_ref[...])
        pre_ref[rows, :] = pre
        gate = jax.nn.sigmoid(pre)
        hidden = (frames_ref[t].astype(F32) + pre * gate).astype(BF)
        for i in range(patch // group):
            sent_ref[i, 0, t] = hidden[i * group : (i + 1) * group]
            sent_ref[i, 1, t] = cot_ref[t, i * group : (i + 1) * group]


def conv_forward(frames, cotangent, low, high, picks, w_conv, parts):
    frames_here, patch, width = frames.shape
    rows = frames_here * patch
    return pl.pallas_call(
        conv_forward_kernel,
        out_shape=(
            pltpu.VMEM((parts, 2, frames_here, patch // parts, width), BF),
            pltpu.VMEM((rows, width), F32),
            pltpu.VMEM((rows, w_conv.shape[0]), BF),
        ),
        name="conv_forward",
        compiler_params=LIMIT,
    )(here(frames), here(cotangent), here(low), here(high), here(picks), here(w_conv))


def attention_kernel(came_ref, w_ref, back_ref, parts_ref):
    parts, _, frames_here, group, width = came_ref.shape
    frames_all = parts * frames_here
    rows_all = frames_all * group
    head_dim = width // HEADS
    scaling = head_dim ** (-0.5)
    half = 8
    rows = frames_all * half
    hidden = came_ref[:, 0].reshape(rows_all, width)
    grads = came_ref[:, 1].reshape(rows_all, width)

    def halves(values):
        cube = values.reshape(frames_all, group, width)
        return [cube[:, s : s + half].reshape(rows, width) for s in range(0, group, half)]

    query = halves(mm(hidden, w_ref[0]))
    key = halves(mm(hidden, w_ref[1]))
    value = halves(mm(hidden, w_ref[2]))
    grad_out = halves(mm_nt(grads, w_ref[3]))
    lane_head = lax.broadcasted_iota(jnp.int32, (rows, width), 1) // head_dim
    same = (
        lax.broadcasted_iota(jnp.int32, (rows, rows), 0) % half
        == lax.broadcasted_iota(jnp.int32, (rows, rows), 1) % half
    )
    same = jnp.where(same, 1.0, 0.0).astype(F32).reshape(1, frames_all, half, rows)

    def spread(values):
        return jnp.concatenate(
            [jnp.where(lane_head == h, values, 0.0).astype(BF) for h in range(HEADS)], axis=0
        )

    def collect(values):
        total = jnp.where(lane_head == 0, values[0:rows], 0.0)
        for h in range(1, HEADS):
            total = jnp.where(lane_head == h, values[h * rows : (h + 1) * rows], total)
        return total

    results = []
    for q32, k32, v32, g32 in zip(query, key, value, grad_out):
        q, g = q32.astype(BF), g32.astype(BF)
        k_heads, v_heads = spread(k32), spread(v32)
        shape4 = (HEADS, frames_all, half, rows)
        scores = mm_nt(k_heads, q).reshape(shape4) * scaling
        expo = jnp.exp(scores - jnp.max(scores, axis=1, keepdims=True))
        probs = expo * (same / jnp.sum(expo, axis=1, keepdims=True))
        probs_b = probs.reshape(-1, rows).astype(BF)
        grad_probs = mm_nt(v_heads, g).reshape(shape4)
        inner = jnp.sum(probs * grad_probs, axis=1, keepdims=True)
        grad_scores = (scaling * probs * (grad_probs - inner)).reshape(-1, rows).astype(BF)
        results.append(
            (
                mm_tn(probs_b, v_heads),
                mm_tn(grad_scores, k_heads),
                collect(mm(grad_scores, q)),
                collect(mm(probs_b, g)),
            )
        )

    def joined(index):
        pieces = [r[index].reshape(frames_all, half, width) for r in results]
        return jnp.concatenate(pieces, axis=1).reshape(rows_all, width).astype(BF)

    attended, grad_query, grad_key, grad_value = (joined(i) for i in range(4))
    back = (
        grads.astype(F32)
        + mm_nt(grad_query, w_ref[0])
        + mm_nt(grad_key, w_ref[1])
        + mm_nt(grad_value, w_ref[2])
    )
    back_ref[...] = back.astype(BF).reshape(back_ref.shape)
    parts_ref[0:width] = mm_tn(hidden, grad_query).astype(parts_ref.dtype)
    parts_ref[1 * width : 2 * width] = mm_tn(hidden, grad_key).astype(parts_ref.dtype)
    parts_ref[2 * width : 3 * width] = mm_tn(hidden, grad_value).astype(parts_ref.dtype)
    parts_ref[3 * width : 4 * width] = mm_tn(attended, grads).astype(parts_ref.dtype)


def attention(came, w_attn):
    parts, _, frames_here, group, width = came.shape
    return pl.pallas_call(
        attention_kernel,
        out_shape=(
            pltpu.VMEM((parts, frames_here, group, width), BF),
            pltpu.VMEM((4 * width, width), BF),
        ),
        name="attention",
        compiler_params=LIMIT,
    )(here(came), w_attn)


def conv_backward_kernel(
    back_ref,
    pre_ref,
    gathered_ref,
    table_ref,
    w_ref,
    attn_ref,
    local_ref,
    low_ref,
    high_ref,
    kept_ref,
    given_ref,
):
    parts, frames_here, group, width = back_ref.shape
    patch = parts * group
    stencil = table_ref.shape[0]
    places = slot_places(table_ref[...])
    target = lax.broadcasted_iota(jnp.int32, (patch + 2 * HW, patch), 0).astype(F32)
    puts = jnp.concatenate(
        [jnp.where(target == places[j : j + 1], 1.0, 0.0).astype(BF) for j in range(stencil)],
        axis=1,
    )
    pre = pre_ref[...]
    gate = jax.nn.sigmoid(pre)
    slope = gate * (1.0 + pre * (1.0 - gate))
    backs, grads = [], []
    for t in range(frames_here):
        back = jnp.concatenate([back_ref[i, t] for i in range(parts)], axis=0).astype(F32)
        backs.append(back)
        grads.append((back * slope[t * patch : (t + 1) * patch]).astype(BF))
    for t in range(frames_here):
        spread = mm_nt(grads[t], w_ref[...]).astype(BF)
        stacked = jnp.concatenate(
            [spread[:, j * width : (j + 1) * width] for j in range(stencil)], axis=0
        )
        extended = mm(puts, stacked)
        low_ref[t] = extended[0:HW].astype(low_ref.dtype)
        high_ref[t] = extended[patch + HW :].astype(high_ref.dtype)
        local_ref[t] = backs[t] + extended[HW : HW + patch]
    grad_pre = jnp.concatenate(grads, axis=0)
    grad_w = mm_tn(gathered_ref[...], grad_pre).astype(BF)
    near = kept_ref.shape[0]
    conv_rows = grad_w.shape[0] // (2 * near)
    attn_rows = attn_ref.shape[0] // (2 * near)
    first = lax.axis_index(PAIR) == 0
    for i in range(near):
        for source, rows, start in ((grad_w, conv_rows, 0), (attn_ref, attn_rows, conv_rows)):
            lower = source[i * rows : (i + 1) * rows]
            upper = source[(near + i) * rows : (near + i + 1) * rows]
            kept_ref[i, start : start + rows] = jnp.where(first, lower, upper)
            given_ref[i, start : start + rows] = jnp.where(first, upper, lower)


def conv_backward(back, pre, gathered, table, w_conv, attn_parts, near):
    parts, frames_here, group, width = back.shape
    patch = parts * group
    weight_rows = (w_conv.shape[0] + attn_parts.shape[0]) // (2 * near)
    return pl.pallas_call(
        conv_backward_kernel,
        out_shape=(
            pltpu.VMEM((frames_here, patch, width), F32),
            pltpu.VMEM((frames_here, HW, width), BF),
            pltpu.VMEM((frames_here, HW, width), BF),
            pltpu.VMEM((near, weight_rows, width), BF),
            pltpu.VMEM((near, weight_rows, width), BF),
        ),
        name="conv_backward",
        compiler_params=LIMIT,
    )(here(back), here(pre), here(gathered), here(table), here(w_conv), here(attn_parts))


LANES = 128


def pair_sum_kernel(kept_ref, came_ref, sum_ref):
    sum_ref[...] = (kept_ref[...].astype(F32) + came_ref[...].astype(F32)).astype(BF)


def pair_sum(kept, came):
    return pl.pallas_call(
        pair_sum_kernel,
        out_shape=pltpu.VMEM(kept.shape, BF),
        name="pair_sum",
        compiler_params=LIMIT,
    )(here(kept), here(came))


def first_sum_kernel(came_ref, tiles_ref):
    total = came_ref[0].astype(F32)
    for i in range(1, came_ref.shape[0]):
        total = total + came_ref[i].astype(F32)
    total = total.astype(BF)
    columns = total.shape[1] // LANES
    count = total.shape[0] // TILE * columns
    for n in range(count):
        row, lane = n // columns * TILE, n % columns * LANES
        tiles_ref[n] = total[row : row + TILE, lane : lane + LANES]
    rest = tiles_ref.shape[0] - count
    if rest:
        tiles_ref[count:] = jnp.zeros((rest, TILE, LANES), BF)


def first_sum(came, tiles):
    return pl.pallas_call(
        first_sum_kernel,
        out_shape=pltpu.VMEM((tiles, TILE, LANES), BF),
        name="first_sum",
        compiler_params=LIMIT,
    )(here(came))


def second_sum_kernel(scaling, came_ref, copies_ref):
    total = (jnp.sum(came_ref[...].astype(F32), axis=0) * scaling).astype(BF)
    for i in range(copies_ref.shape[0]):
        copies_ref[i] = total


def second_sum(came, scaling):
    return pl.pallas_call(
        functools.partial(second_sum_kernel, scaling),
        out_shape=pltpu.VMEM(came.shape, BF),
        name="second_sum",
        compiler_params=LIMIT,
    )(here(came))


def untile_kernel(tiles_ref, copies_ref):
    rows, width = copies_ref.shape[1:]
    columns = width // LANES
    for n in range(rows // TILE * columns):
        row, lane = n // columns * TILE, n % columns * LANES
        tile = tiles_ref[n]
        for i in range(copies_ref.shape[0]):
            copies_ref[i, row : row + TILE, lane : lane + LANES] = tile


def untile(tiles, shape):
    return pl.pallas_call(
        untile_kernel, out_shape=pltpu.VMEM(shape, BF), name="untile", compiler_params=LIMIT
    )(here(tiles))


def unpack_kernel(own_ref, other_ref, conv_ref, attn_ref, sem):
    conv_rows = conv_ref.shape[2]
    mine = lax.axis_index(PAIR)
    moves = []
    for n, (ref, half) in enumerate(((own_ref, mine), (other_ref, 1 - mine))):
        moves.append(
            pltpu.make_async_copy(ref.at[:, 0:conv_rows], conv_ref.at[half], sem.at[n, 0])
        )
        moves.append(
            pltpu.make_async_copy(ref.at[:, conv_rows:], attn_ref.at[half], sem.at[n, 1])
        )
    for move in moves:
        move.start()
    for move in moves:
        move.wait()


def unpack(own, other, conv_rows, attn_rows):
    near, _, width = own.shape
    return pl.pallas_call(
        unpack_kernel,
        out_shape=(
            jax.ShapeDtypeStruct((2, near, conv_rows // (2 * near), width), BF),
            jax.ShapeDtypeStruct((2, near, attn_rows // (2 * near), width), BF),
        ),
        in_specs=[pl.BlockSpec(memory_space=pltpu.VMEM)] * 2,
        out_specs=[pl.BlockSpec(memory_space=pl.ANY)] * 2,
        scratch_shapes=[pltpu.SemaphoreType.DMA((2, 2))],
        name="unpack",
        compiler_params=LIMIT,
    )(here(own), here(other))


def exchange(values, axis):
    return lax.all_to_all(values, axis, 0, 0, tiled=True)


def far_off(values):
    return pltpu.with_memory_space_constraint(values, pltpu.HBM)


def here(values):
    return pltpu.with_memory_space_constraint(values, pltpu.VMEM)


def to_neighbours(upward, downward):
    count = lax.axis_size(VERT)
    steps = [(i, i + 1) for i in range(count - 1)]
    from_below = lax.ppermute(upward, VERT, steps)
    from_above = lax.ppermute(downward, VERT, [(b, a) for a, b in steps])
    return from_below, from_above


def swap(values):
    return lax.ppermute(values, PAIR, [(0, 1), (1, 0)])


def body(frames, cotangent, table, w_conv, w_attn):
    _, patch, _ = frames.shape
    parts = lax.axis_size(TM)
    patches = lax.axis_size(VERT)
    near, far = lax.axis_size(NEAR), lax.axis_size(FAR)
    low, high = to_neighbours(frames[:, patch - HW :], frames[:, :HW])
    frames, cotangent, table, w_conv, picks = stage(frames, cotangent, table.T, w_conv)
    sent, pre, gathered = conv_forward(frames, cotangent, low, high, picks, w_conv, parts)
    back_time, attn_parts = attention(exchange(sent, TM), w_attn)
    back = exchange(back_time, TM)
    local, rim_low, rim_high, kept, given = conv_backward(
        back, pre, gathered, table, w_conv, attn_parts, near
    )
    came = swap(given)
    from_below, from_above = to_neighbours(rim_high, rim_low)
    weights = pair_sum(kept, came)
    arrived = jnp.concatenate([from_below, from_above], axis=1).astype(F32)
    grad_frames = (local + arrived).astype(BF)
    count = weights[0].size // (TILE * LANES)
    each = -(-count // far)
    came = exchange(weights, NEAR)
    tiles = first_sum(came, each * far)
    scaling = 1.0 / math.sqrt(TF * patch * patches)
    came = exchange(tiles, FAR).reshape(far, each, TILE, LANES)
    copies = second_sum(came, scaling).reshape(tiles.shape)
    copies = untile(exchange(copies, FAR), weights.shape)
    own = exchange(copies, NEAR)
    grad_conv, grad_attn = unpack(own, swap(own), w_conv.shape[0], attn_parts.shape[0])
    return grad_frames, grad_conv.reshape(w_conv.shape), grad_attn.reshape(w_attn.shape)


def solution(mesh):
    parts, patches = mesh.devices.shape
    sizes = (parts // 4, 2, 2, patches // 16, 2, 2, 2, 2)
    fine = jax.sharding.Mesh(mesh.devices.reshape(sizes), TM + VERT)
    return jax.shard_map(
        body,
        mesh=fine,
        in_specs=(P(TM, VERT, None), P(TM, VERT, None), P(VERT, None), P(), P()),
        out_specs=(P(TM, VERT, None), P(), P()),
        check_vma=False,
    )
```

```python
import functools
import itertools
import math

import jax
import jax.numpy as jnp
from jax import lax
from jax.experimental import pallas as pl
from jax.experimental.pallas import tpu as pltpu
from jax.sharding import PartitionSpec as P


TF = 16
HEADS = 8
HW = 64
TM = ("x_hi", "x_lo", "z_hi")
VERT = ("y_hi", "y_lo", "z_mid", "z_lo", "core")
PAIR = "core"
NEAR = ("x_lo", "y_lo", "z_lo")
FAR = ("x_hi", "z_hi", "y_hi", "z_mid")
TILE = 16
BF = jnp.bfloat16
F32 = jnp.float32

LIMIT = pltpu.CompilerParams(vmem_limit_bytes=32 * 1024 * 1024)


def mm(left, right):
    return jnp.dot(left, right, preferred_element_type=F32)


def mm_nt(left, right):
    return lax.dot_general(left, right, (((1,), (1,)), ((), ())), preferred_element_type=F32)


def mm_tn(left, right):
    return lax.dot_general(left, right, (((0,), (0,)), ((), ())), preferred_element_type=F32)


def slot_places(table):
    lanes = lax.broadcasted_iota(jnp.int32, table.shape, 1)
    return jnp.where(table < 0, -1, table - table[0:1] + lanes + HW).astype(F32)


def stage_kernel(
    frames_ref, cot_ref, table_ref, w_ref, frames_out, cot_out, table_out, w_out, picks_ref, sem
):
    pairs = (
        (table_ref, table_out),
        (w_ref, w_out),
        (frames_ref, frames_out),
        (cot_ref, cot_out),
    )
    moves = [pltpu.make_async_copy(a, b, sem.at[i]) for i, (a, b) in enumerate(pairs)]
    for move in moves:
        move.start()
    moves[0].wait()
    stencil, patch = table_out.shape
    places = slot_places(table_out[...])
    row = lax.broadcasted_iota(jnp.int32, (patch, patch), 0)
    square = jnp.full((patch, patch), -1.0, F32)
    for j in range(1, stencil):
        square = jnp.where(row == j, places[j : j + 1], square)
    columns = square.T
    lanes = lax.broadcasted_iota(jnp.int32, (patch, patch + 2 * HW), 1).astype(F32)
    for j in range(1, stencil):
        picks_ref[(j - 1) * patch : j * patch, :] = jnp.where(
            lanes == columns[:, j : j + 1], 1.0, 0.0
        ).astype(BF)
    for move in moves[1:]:
        move.wait()


def stage(frames, cotangent, table, w_conv):
    stencil, patch = table.shape
    return pl.pallas_call(
        stage_kernel,
        out_shape=(
            pltpu.VMEM(frames.shape, BF),
            pltpu.VMEM(cotangent.shape, BF),
            pltpu.VMEM(table.shape, jnp.int32),
            pltpu.VMEM(w_conv.shape, BF),
            pltpu.VMEM(((stencil - 1) * patch, patch + 2 * HW), BF),
        ),
        in_specs=[pl.BlockSpec(memory_space=pl.ANY)] * 4,
        scratch_shapes=[pltpu.SemaphoreType.DMA((4,))],
        name="stage",
        compiler_params=LIMIT,
    )(*(far_off(x) for x in (frames, cotangent, table, w_conv)))


def conv_forward_kernel(
    frames_ref, cot_ref, low_ref, high_ref, picks_ref, w_ref, sent_ref, pre_ref, gathered_ref
):
    frames_here, patch, width = frames_ref.shape
    stencil = picks_ref.shape[0] // patch + 1
    group = sent_ref.shape[3]
    for t in range(frames_here):
        rows = pl.ds(t * patch, patch)
        extended = jnp.concatenate([low_ref[t], frames_ref[t], high_ref[t]], axis=0)
        taken = mm(picks_ref[...], extended).astype(BF)
        gathered_ref[rows, 0:width] = frames_ref[t]
        for j in range(1, stencil):
            gathered_ref[rows, j * width : (j + 1) * width] = taken[(j - 1) * patch : j * patch]
        pre = mm(gathered_ref[rows, :], w_ref[...])
        pre_ref[rows, :] = pre
        gate = jax.nn.sigmoid(pre)
        hidden = (frames_ref[t].astype(F32) + pre * gate).astype(BF)
        for i in range(patch // group):
            sent_ref[i, 0, t] = hidden[i * group : (i + 1) * group]
            sent_ref[i, 1, t] = cot_ref[t, i * group : (i + 1) * group]


def conv_forward(frames, cotangent, low, high, picks, w_conv, parts):
    frames_here, patch, width = frames.shape
    rows = frames_here * patch
    return pl.pallas_call(
        conv_forward_kernel,
        out_shape=(
            pltpu.VMEM((parts, 2, frames_here, patch // parts, width), BF),
            pltpu.VMEM((rows, width), F32),
            pltpu.VMEM((rows, w_conv.shape[0]), BF),
        ),
        name="conv_forward",
        compiler_params=LIMIT,
    )(here(frames), here(cotangent), here(low), here(high), here(picks), here(w_conv))


def attention_kernel(came_ref, w_ref, back_ref, parts_ref):
    parts, _, frames_here, group, width = came_ref.shape
    frames_all = parts * frames_here
    rows_all = frames_all * group
    head_dim = width // HEADS
    scaling = head_dim ** (-0.5)
    half = 8
    rows = frames_all * half
    hidden = came_ref[:, 0].reshape(rows_all, width)
    grads = came_ref[:, 1].reshape(rows_all, width)

    def halves(values):
        cube = values.reshape(frames_all, group, width)
        return [cube[:, s : s + half].reshape(rows, width) for s in range(0, group, half)]

    query = halves(mm(hidden, w_ref[0]))
    key = halves(mm(hidden, w_ref[1]))
    value = halves(mm(hidden, w_ref[2]))
    grad_out = halves(mm_nt(grads, w_ref[3]))
    lane_head = lax.broadcasted_iota(jnp.int32, (rows, width), 1) // head_dim
    same = (
        lax.broadcasted_iota(jnp.int32, (rows, rows), 0) % half
        == lax.broadcasted_iota(jnp.int32, (rows, rows), 1) % half
    )
    same = jnp.where(same, 1.0, 0.0).astype(F32).reshape(1, frames_all, half, rows)

    def spread(values):
        return jnp.concatenate(
            [jnp.where(lane_head == h, values, 0.0).astype(BF) for h in range(HEADS)], axis=0
        )

    def collect(values):
        total = jnp.where(lane_head == 0, values[0:rows], 0.0)
        for h in range(1, HEADS):
            total = jnp.where(lane_head == h, values[h * rows : (h + 1) * rows], total)
        return total

    results = []
    for q32, k32, v32, g32 in zip(query, key, value, grad_out):
        q, g = q32.astype(BF), g32.astype(BF)
        k_heads, v_heads = spread(k32), spread(v32)
        shape4 = (HEADS, frames_all, half, rows)
        scores = mm_nt(k_heads, q).reshape(shape4) * scaling
        expo = jnp.exp(scores - jnp.max(scores, axis=1, keepdims=True))
        probs = expo * (same / jnp.sum(expo, axis=1, keepdims=True))
        probs_b = probs.reshape(-1, rows).astype(BF)
        grad_probs = mm_nt(v_heads, g).reshape(shape4)
        inner = jnp.sum(probs * grad_probs, axis=1, keepdims=True)
        grad_scores = (scaling * probs * (grad_probs - inner)).reshape(-1, rows).astype(BF)
        results.append(
            (
                mm_tn(probs_b, v_heads),
                mm_tn(grad_scores, k_heads),
                collect(mm(grad_scores, q)),
                collect(mm(probs_b, g)),
            )
        )

    def joined(index):
        pieces = [r[index].reshape(frames_all, half, width) for r in results]
        return jnp.concatenate(pieces, axis=1).reshape(rows_all, width).astype(BF)

    attended, grad_query, grad_key, grad_value = (joined(i) for i in range(4))
    back = (
        grads.astype(F32)
        + mm_nt(grad_query, w_ref[0])
        + mm_nt(grad_key, w_ref[1])
        + mm_nt(grad_value, w_ref[2])
    )
    back_ref[...] = back.astype(BF).reshape(back_ref.shape)
    parts_ref[0:width] = mm_tn(hidden, grad_query).astype(parts_ref.dtype)
    parts_ref[1 * width : 2 * width] = mm_tn(hidden, grad_key).astype(parts_ref.dtype)
    parts_ref[2 * width : 3 * width] = mm_tn(hidden, grad_value).astype(parts_ref.dtype)
    parts_ref[3 * width : 4 * width] = mm_tn(attended, grads).astype(parts_ref.dtype)


def attention(came, w_attn):
    parts, _, frames_here, group, width = came.shape
    return pl.pallas_call(
        attention_kernel,
        out_shape=(
            pltpu.VMEM((parts, frames_here, group, width), BF),
            pltpu.VMEM((4 * width, width), BF),
        ),
        name="attention",
        compiler_params=LIMIT,
    )(here(came), w_attn)


def conv_backward_kernel(
    back_ref,
    pre_ref,
    gathered_ref,
    table_ref,
    w_ref,
    attn_ref,
    local_ref,
    low_ref,
    high_ref,
    kept_ref,
    given_ref,
):
    parts, frames_here, group, width = back_ref.shape
    patch = parts * group
    stencil = table_ref.shape[0]
    places = slot_places(table_ref[...])
    target = lax.broadcasted_iota(jnp.int32, (patch + 2 * HW, patch), 0).astype(F32)
    puts = jnp.concatenate(
        [jnp.where(target == places[j : j + 1], 1.0, 0.0).astype(BF) for j in range(stencil)],
        axis=1,
    )
    pre = pre_ref[...]
    gate = jax.nn.sigmoid(pre)
    slope = gate * (1.0 + pre * (1.0 - gate))
    backs, grads = [], []
    for t in range(frames_here):
        back = jnp.concatenate([back_ref[i, t] for i in range(parts)], axis=0).astype(F32)
        backs.append(back)
        grads.append((back * slope[t * patch : (t + 1) * patch]).astype(BF))
    for t in range(frames_here):
        spread = mm_nt(grads[t], w_ref[...]).astype(BF)
        stacked = jnp.concatenate(
            [spread[:, j * width : (j + 1) * width] for j in range(stencil)], axis=0
        )
        extended = mm(puts, stacked)
        low_ref[t] = extended[0:HW].astype(low_ref.dtype)
        high_ref[t] = extended[patch + HW :].astype(high_ref.dtype)
        local_ref[t] = backs[t] + extended[HW : HW + patch]
    grad_pre = jnp.concatenate(grads, axis=0)
    grad_w = mm_tn(gathered_ref[...], grad_pre).astype(BF)
    near = kept_ref.shape[0]
    conv_rows = grad_w.shape[0] // (2 * near)
    attn_rows = attn_ref.shape[0] // (2 * near)
    first = lax.axis_index(PAIR) == 0
    for i in range(near):
        for source, rows, start in ((grad_w, conv_rows, 0), (attn_ref, attn_rows, conv_rows)):
            lower = source[i * rows : (i + 1) * rows]
            upper = source[(near + i) * rows : (near + i + 1) * rows]
            kept_ref[i, start : start + rows] = jnp.where(first, lower, upper)
            given_ref[i, start : start + rows] = jnp.where(first, upper, lower)


def conv_backward(back, pre, gathered, table, w_conv, attn_parts, near):
    parts, frames_here, group, width = back.shape
    patch = parts * group
    weight_rows = (w_conv.shape[0] + attn_parts.shape[0]) // (2 * near)
    return pl.pallas_call(
        conv_backward_kernel,
        out_shape=(
            pltpu.VMEM((frames_here, patch, width), F32),
            pltpu.VMEM((frames_here, HW, width), BF),
            pltpu.VMEM((frames_here, HW, width), BF),
            pltpu.VMEM((near, weight_rows, width), BF),
            pltpu.VMEM((near, weight_rows, width), BF),
        ),
        name="conv_backward",
        compiler_params=LIMIT,
    )(here(back), here(pre), here(gathered), here(table), here(w_conv), here(attn_parts))


LANES = 128


def pair_sum_kernel(kept_ref, came_ref, sum_ref):
    sum_ref[...] = (kept_ref[...].astype(F32) + came_ref[...].astype(F32)).astype(BF)


def pair_sum(kept, came):
    return pl.pallas_call(
        pair_sum_kernel,
        out_shape=pltpu.VMEM(kept.shape, BF),
        name="pair_sum",
        compiler_params=LIMIT,
    )(here(kept), here(came))


def first_sum_kernel(came_ref, tiles_ref):
    total = came_ref[0].astype(F32)
    for i in range(1, came_ref.shape[0]):
        total = total + came_ref[i].astype(F32)
    total = total.astype(BF)
    columns = total.shape[1] // LANES
    count = total.shape[0] // TILE * columns
    for n in range(count):
        row, lane = n // columns * TILE, n % columns * LANES
        tiles_ref[n] = total[row : row + TILE, lane : lane + LANES]
    rest = tiles_ref.shape[0] - count
    if rest:
        tiles_ref[count:] = jnp.zeros((rest, TILE, LANES), BF)


def first_sum(came, tiles):
    return pl.pallas_call(
        first_sum_kernel,
        out_shape=pltpu.VMEM((tiles, TILE, LANES), BF),
        name="first_sum",
        compiler_params=LIMIT,
    )(here(came))


def second_sum_kernel(scaling, came_ref, copies_ref):
    total = (jnp.sum(came_ref[...].astype(F32), axis=0) * scaling).astype(BF)
    for i in range(copies_ref.shape[0]):
        copies_ref[i] = total


def second_sum(came, scaling):
    return pl.pallas_call(
        functools.partial(second_sum_kernel, scaling),
        out_shape=pltpu.VMEM(came.shape, BF),
        name="second_sum",
        compiler_params=LIMIT,
    )(here(came))


def untile_kernel(tiles_ref, copies_ref):
    rows, width = copies_ref.shape[1:]
    columns = width // LANES
    for n in range(rows // TILE * columns):
        row, lane = n // columns * TILE, n % columns * LANES
        tile = tiles_ref[n]
        for i in range(copies_ref.shape[0]):
            copies_ref[i, row : row + TILE, lane : lane + LANES] = tile


def untile(tiles, shape):
    return pl.pallas_call(
        untile_kernel, out_shape=pltpu.VMEM(shape, BF), name="untile", compiler_params=LIMIT
    )(here(tiles))


def unpack_kernel(own_ref, other_ref, conv_ref, attn_ref, sem):
    conv_rows = conv_ref.shape[2]
    mine = lax.axis_index(PAIR)
    moves = []
    for n, (ref, half) in enumerate(((own_ref, mine), (other_ref, 1 - mine))):
        moves.append(
            pltpu.make_async_copy(ref.at[:, 0:conv_rows], conv_ref.at[half], sem.at[n, 0])
        )
        moves.append(
            pltpu.make_async_copy(ref.at[:, conv_rows:], attn_ref.at[half], sem.at[n, 1])
        )
    for move in moves:
        move.start()
    for move in moves:
        move.wait()


def unpack(own, other, conv_rows, attn_rows):
    near, _, width = own.shape
    return pl.pallas_call(
        unpack_kernel,
        out_shape=(
            jax.ShapeDtypeStruct((2, near, conv_rows // (2 * near), width), BF),
            jax.ShapeDtypeStruct((2, near, attn_rows // (2 * near), width), BF),
        ),
        in_specs=[pl.BlockSpec(memory_space=pltpu.VMEM)] * 2,
        out_specs=[pl.BlockSpec(memory_space=pl.ANY)] * 2,
        scratch_shapes=[pltpu.SemaphoreType.DMA((2, 2))],
        name="unpack",
        compiler_params=LIMIT,
    )(here(own), here(other))


def exchange(values, axis):
    return lax.all_to_all(values, axis, 0, 0, tiled=True)


def near_groups():
    x_hi, x_lo, z_hi, y_hi, y_lo, z_mid, z_lo, cores = (lax.axis_size(a) for a in TM + VERT)
    ends = (x_hi * x_lo, y_hi * y_lo, z_hi * z_mid * z_lo)
    steps = (x_lo, y_lo, z_lo)
    groups = []
    for core in range(cores):
        for corner in itertools.product(*(range(0, e, s) for e, s in zip(ends, steps))):
            group = []
            for parity in itertools.product(*(range(s) for s in steps)):
                x, y, z = (
                    (c + p + (core * s if p == 0 else 0)) % e
                    for c, p, s, e in zip(corner, parity, steps, ends)
                )
                z_far, z_near = divmod(z, z_mid * z_lo)
                place = ((x * z_hi + z_far) * ends[1] + y) * z_mid * z_lo + z_near
                group.append(place * cores + core)
            groups.append(group)
    return groups


def near_exchange(values):
    return lax.all_to_all(
        values, TM + VERT, 0, 0, axis_index_groups=near_groups(), tiled=True
    )


def far_off(values):
    return pltpu.with_memory_space_constraint(values, pltpu.HBM)


def here(values):
    return pltpu.with_memory_space_constraint(values, pltpu.VMEM)


def to_neighbours(upward, downward):
    count = lax.axis_size(VERT)
    steps = [(i, i + 1) for i in range(count - 1)]
    from_below = lax.ppermute(upward, VERT, steps)
    from_above = lax.ppermute(downward, VERT, [(b, a) for a, b in steps])
    return from_below, from_above


def swap(values):
    return lax.ppermute(values, PAIR, [(0, 1), (1, 0)])


def body(frames, cotangent, table, w_conv, w_attn):
    _, patch, _ = frames.shape
    parts = lax.axis_size(TM)
    patches = lax.axis_size(VERT)
    near, far = lax.axis_size(NEAR), lax.axis_size(FAR)
    low, high = to_neighbours(frames[:, patch - HW :], frames[:, :HW])
    frames, cotangent, table, w_conv, picks = stage(frames, cotangent, table.T, w_conv)
    sent, pre, gathered = conv_forward(frames, cotangent, low, high, picks, w_conv, parts)
    back_time, attn_parts = attention(exchange(sent, TM), w_attn)
    back = exchange(back_time, TM)
    local, rim_low, rim_high, kept, given = conv_backward(
        back, pre, gathered, table, w_conv, attn_parts, near
    )
    came = swap(given)
    from_below, from_above = to_neighbours(rim_high, rim_low)
    weights = pair_sum(kept, came)
    arrived = jnp.concatenate([from_below, from_above], axis=1).astype(F32)
    grad_frames = (local + arrived).astype(BF)
    count = weights[0].size // (TILE * LANES)
    each = -(-count // far)
    came = near_exchange(weights)
    tiles = first_sum(came, each * far)
    scaling = 1.0 / math.sqrt(TF * patch * patches)
    came = exchange(tiles, FAR).reshape(far, each, TILE, LANES)
    copies = second_sum(came, scaling).reshape(tiles.shape)
    copies = untile(exchange(copies, FAR), weights.shape)
    own = near_exchange(copies)
    grad_conv, grad_attn = unpack(own, swap(own), w_conv.shape[0], attn_parts.shape[0])
    return grad_frames, grad_conv.reshape(w_conv.shape), grad_attn.reshape(w_attn.shape)


def solution(mesh):
    parts, patches = mesh.devices.shape
    sizes = (parts // 4, 2, 2, patches // 16, 2, 2, 2, 2)
    fine = jax.sharding.Mesh(mesh.devices.reshape(sizes), TM + VERT)
    return jax.shard_map(
        body,
        mesh=fine,
        in_specs=(P(TM, VERT, None), P(TM, VERT, None), P(VERT, None), P(), P()),
        out_specs=(P(TM, VERT, None), P(), P()),
        check_vma=False,
    )
```

```python
import functools
import math

import jax
import jax.numpy as jnp
from jax import lax
from jax.experimental import pallas as pl
from jax.experimental.pallas import tpu as pltpu
from jax.sharding import PartitionSpec as P


TF = 16
HEADS = 8
HW = 64
TM = ("x_hi", "x_lo", "z_hi")
VERT = ("y_hi", "y_lo", "z_mid", "z_lo", "core")
PAIR = "core"
NEAR = ("x_lo", "y_lo", "z_lo")
LINE = ("z_hi", "z_mid")
PLANE = ("x_hi", "y_hi")
TILE = 16
BF = jnp.bfloat16
F32 = jnp.float32

LIMIT = pltpu.CompilerParams(vmem_limit_bytes=32 * 1024 * 1024)


def mm(left, right):
    return jnp.dot(left, right, preferred_element_type=F32)


def mm_nt(left, right):
    return lax.dot_general(left, right, (((1,), (1,)), ((), ())), preferred_element_type=F32)


def mm_tn(left, right):
    return lax.dot_general(left, right, (((0,), (0,)), ((), ())), preferred_element_type=F32)


def slot_places(table):
    lanes = lax.broadcasted_iota(jnp.int32, table.shape, 1)
    return jnp.where(table < 0, -1, table - table[0:1] + lanes + HW).astype(F32)


def stage_kernel(
    frames_ref, cot_ref, table_ref, w_ref, frames_out, cot_out, table_out, w_out, picks_ref, sem
):
    pairs = (
        (table_ref, table_out),
        (w_ref, w_out),
        (frames_ref, frames_out),
        (cot_ref, cot_out),
    )
    moves = [pltpu.make_async_copy(a, b, sem.at[i]) for i, (a, b) in enumerate(pairs)]
    for move in moves:
        move.start()
    moves[0].wait()
    stencil, patch = table_out.shape
    places = slot_places(table_out[...])
    row = lax.broadcasted_iota(jnp.int32, (patch, patch), 0)
    square = jnp.full((patch, patch), -1.0, F32)
    for j in range(1, stencil):
        square = jnp.where(row == j, places[j : j + 1], square)
    columns = square.T
    lanes = lax.broadcasted_iota(jnp.int32, (patch, patch + 2 * HW), 1).astype(F32)
    for j in range(1, stencil):
        picks_ref[(j - 1) * patch : j * patch, :] = jnp.where(
            lanes == columns[:, j : j + 1], 1.0, 0.0
        ).astype(BF)
    for move in moves[1:]:
        move.wait()


def stage(frames, cotangent, table, w_conv):
    stencil, patch = table.shape
    return pl.pallas_call(
        stage_kernel,
        out_shape=(
            pltpu.VMEM(frames.shape, BF),
            pltpu.VMEM(cotangent.shape, BF),
            pltpu.VMEM(table.shape, jnp.int32),
            pltpu.VMEM(w_conv.shape, BF),
            pltpu.VMEM(((stencil - 1) * patch, patch + 2 * HW), BF),
        ),
        in_specs=[pl.BlockSpec(memory_space=pl.ANY)] * 4,
        scratch_shapes=[pltpu.SemaphoreType.DMA((4,))],
        name="stage",
        compiler_params=LIMIT,
    )(*(far_off(x) for x in (frames, cotangent, table, w_conv)))


def conv_forward_kernel(
    frames_ref, cot_ref, outer_ref, inner_ref, picks_ref, w_ref, sent_ref, pre_ref, gathered_ref
):
    frames_here, patch, width = frames_ref.shape
    stencil = picks_ref.shape[0] // patch + 1
    group = sent_ref.shape[3]
    first = lax.axis_index(PAIR) == 0
    for t in range(frames_here):
        rows = pl.ds(t * patch, patch)
        low = jnp.where(first, outer_ref[t], inner_ref[t])
        high = jnp.where(first, inner_ref[t], outer_ref[t])
        extended = jnp.concatenate([low, frames_ref[t], high], axis=0)
        taken = mm(picks_ref[...], extended).astype(BF)
        gathered_ref[rows, 0:width] = frames_ref[t]
        for j in range(1, stencil):
            gathered_ref[rows, j * width : (j + 1) * width] = taken[(j - 1) * patch : j * patch]
        pre = mm(gathered_ref[rows, :], w_ref[...])
        pre_ref[rows, :] = pre
        gate = jax.nn.sigmoid(pre)
        hidden = (frames_ref[t].astype(F32) + pre * gate).astype(BF)
        for i in range(patch // group):
            sent_ref[i, 0, t] = hidden[i * group : (i + 1) * group]
            sent_ref[i, 1, t] = cot_ref[t, i * group : (i + 1) * group]


def conv_forward(frames, cotangent, outer, inner, picks, w_conv, parts):
    frames_here, patch, width = frames.shape
    rows = frames_here * patch
    return pl.pallas_call(
        conv_forward_kernel,
        out_shape=(
            pltpu.VMEM((parts, 2, frames_here, patch // parts, width), BF),
            pltpu.VMEM((rows, width), F32),
            pltpu.VMEM((rows, w_conv.shape[0]), BF),
        ),
        name="conv_forward",
        compiler_params=LIMIT,
    )(here(frames), here(cotangent), here(outer), here(inner), here(picks), here(w_conv))


def attention_kernel(came_ref, w_ref, back_ref, parts_ref):
    parts, _, frames_here, group, width = came_ref.shape
    frames_all = parts * frames_here
    rows_all = frames_all * group
    head_dim = width // HEADS
    scaling = head_dim ** (-0.5)
    half = 8
    rows = frames_all * half
    hidden = came_ref[:, 0].reshape(rows_all, width)
    grads = came_ref[:, 1].reshape(rows_all, width)

    def halves(values):
        cube = values.reshape(frames_all, group, width)
        return [cube[:, s : s + half].reshape(rows, width) for s in range(0, group, half)]

    query = halves(mm(hidden, w_ref[0]))
    key = halves(mm(hidden, w_ref[1]))
    value = halves(mm(hidden, w_ref[2]))
    grad_out = halves(mm_nt(grads, w_ref[3]))
    lane_head = lax.broadcasted_iota(jnp.int32, (rows, width), 1) // head_dim
    same = (
        lax.broadcasted_iota(jnp.int32, (rows, rows), 0) % half
        == lax.broadcasted_iota(jnp.int32, (rows, rows), 1) % half
    )
    same = jnp.where(same, 1.0, 0.0).astype(F32).reshape(1, frames_all, half, rows)

    def spread(values):
        return jnp.concatenate(
            [jnp.where(lane_head == h, values, 0.0).astype(BF) for h in range(HEADS)], axis=0
        )

    def collect(values):
        total = jnp.where(lane_head == 0, values[0:rows], 0.0)
        for h in range(1, HEADS):
            total = jnp.where(lane_head == h, values[h * rows : (h + 1) * rows], total)
        return total

    results = []
    for q32, k32, v32, g32 in zip(query, key, value, grad_out):
        q, g = q32.astype(BF), g32.astype(BF)
        k_heads, v_heads = spread(k32), spread(v32)
        shape4 = (HEADS, frames_all, half, rows)
        scores = mm_nt(k_heads, q).reshape(shape4) * scaling
        expo = jnp.exp(scores - jnp.max(scores, axis=1, keepdims=True))
        probs = expo * (same / jnp.sum(expo, axis=1, keepdims=True))
        probs_b = probs.reshape(-1, rows).astype(BF)
        grad_probs = mm_nt(v_heads, g).reshape(shape4)
        inner = jnp.sum(probs * grad_probs, axis=1, keepdims=True)
        grad_scores = (scaling * probs * (grad_probs - inner)).reshape(-1, rows).astype(BF)
        results.append(
            (
                mm_tn(probs_b, v_heads),
                mm_tn(grad_scores, k_heads),
                collect(mm(grad_scores, q)),
                collect(mm(probs_b, g)),
            )
        )

    def joined(index):
        pieces = [r[index].reshape(frames_all, half, width) for r in results]
        return jnp.concatenate(pieces, axis=1).reshape(rows_all, width).astype(BF)

    attended, grad_query, grad_key, grad_value = (joined(i) for i in range(4))
    back = (
        grads.astype(F32)
        + mm_nt(grad_query, w_ref[0])
        + mm_nt(grad_key, w_ref[1])
        + mm_nt(grad_value, w_ref[2])
    )
    back_ref[...] = back.astype(BF).reshape(back_ref.shape)
    parts_ref[0:width] = mm_tn(hidden, grad_query).astype(parts_ref.dtype)
    parts_ref[1 * width : 2 * width] = mm_tn(hidden, grad_key).astype(parts_ref.dtype)
    parts_ref[2 * width : 3 * width] = mm_tn(hidden, grad_value).astype(parts_ref.dtype)
    parts_ref[3 * width : 4 * width] = mm_tn(attended, grads).astype(parts_ref.dtype)


def attention(came, w_attn):
    parts, _, frames_here, group, width = came.shape
    return pl.pallas_call(
        attention_kernel,
        out_shape=(
            pltpu.VMEM((parts, frames_here, group, width), BF),
            pltpu.VMEM((4 * width, width), BF),
        ),
        name="attention",
        compiler_params=LIMIT,
    )(here(came), w_attn)


def conv_backward_kernel(
    back_ref,
    pre_ref,
    gathered_ref,
    table_ref,
    w_ref,
    attn_ref,
    local_ref,
    outer_ref,
    inner_ref,
    kept_ref,
    given_ref,
):
    parts, frames_here, group, width = back_ref.shape
    patch = parts * group
    stencil = table_ref.shape[0]
    places = slot_places(table_ref[...])
    target = lax.broadcasted_iota(jnp.int32, (patch + 2 * HW, patch), 0).astype(F32)
    puts = jnp.concatenate(
        [jnp.where(target == places[j : j + 1], 1.0, 0.0).astype(BF) for j in range(stencil)],
        axis=1,
    )
    pre = pre_ref[...]
    gate = jax.nn.sigmoid(pre)
    slope = gate * (1.0 + pre * (1.0 - gate))
    first = lax.axis_index(PAIR) == 0
    backs, grads = [], []
    for t in range(frames_here):
        back = jnp.concatenate([back_ref[i, t] for i in range(parts)], axis=0).astype(F32)
        backs.append(back)
        grads.append((back * slope[t * patch : (t + 1) * patch]).astype(BF))
    for t in range(frames_here):
        spread = mm_nt(grads[t], w_ref[...]).astype(BF)
        stacked = jnp.concatenate(
            [spread[:, j * width : (j + 1) * width] for j in range(stencil)], axis=0
        )
        extended = mm(puts, stacked)
        low, high = extended[0:HW].astype(BF), extended[patch + HW :].astype(BF)
        outer_ref[t] = jnp.where(first, low, high)
        inner_ref[t] = jnp.where(first, high, low)
        local_ref[t] = backs[t] + extended[HW : HW + patch]
    grad_pre = jnp.concatenate(grads, axis=0)
    grad_w = mm_tn(gathered_ref[...], grad_pre).astype(BF)
    near = kept_ref.shape[0]
    conv_rows = grad_w.shape[0] // (2 * near)
    attn_rows = attn_ref.shape[0] // (2 * near)
    for i in range(near):
        for source, rows, start in ((grad_w, conv_rows, 0), (attn_ref, attn_rows, conv_rows)):
            lower = source[i * rows : (i + 1) * rows]
            upper = source[(near + i) * rows : (near + i + 1) * rows]
            kept_ref[i, start : start + rows] = jnp.where(first, lower, upper)
            given_ref[i, start : start + rows] = jnp.where(first, upper, lower)


def conv_backward(back, pre, gathered, table, w_conv, attn_parts, near):
    parts, frames_here, group, width = back.shape
    patch = parts * group
    weight_rows = (w_conv.shape[0] + attn_parts.shape[0]) // (2 * near)
    return pl.pallas_call(
        conv_backward_kernel,
        out_shape=(
            pltpu.VMEM((frames_here, patch, width), F32),
            pltpu.VMEM((frames_here, HW, width), BF),
            pltpu.VMEM((frames_here, HW, width), BF),
            pltpu.VMEM((near, weight_rows, width), BF),
            pltpu.VMEM((near, weight_rows, width), BF),
        ),
        name="conv_backward",
        compiler_params=LIMIT,
    )(here(back), here(pre), here(gathered), here(table), here(w_conv), here(attn_parts))


LANES = 128


def pair_sum_kernel(kept_ref, came_ref, sum_ref):
    sum_ref[...] = (kept_ref[...].astype(F32) + came_ref[...].astype(F32)).astype(BF)


def pair_sum(kept, came):
    return pl.pallas_call(
        pair_sum_kernel,
        out_shape=pltpu.VMEM(kept.shape, BF),
        name="pair_sum",
        compiler_params=LIMIT,
    )(here(kept), here(came))


def first_sum_kernel(came_ref, tiles_ref):
    total = came_ref[0].astype(F32)
    for i in range(1, came_ref.shape[0]):
        total = total + came_ref[i].astype(F32)
    total = total.astype(BF)
    columns = total.shape[1] // LANES
    count = total.shape[0] // TILE * columns
    for n in range(count):
        row, lane = n // columns * TILE, n % columns * LANES
        tiles_ref[n] = total[row : row + TILE, lane : lane + LANES]
    rest = tiles_ref.shape[0] - count
    if rest:
        tiles_ref[count:] = jnp.zeros((rest, TILE, LANES), BF)


def first_sum(came, tiles):
    return pl.pallas_call(
        first_sum_kernel,
        out_shape=pltpu.VMEM((tiles, TILE, LANES), BF),
        name="first_sum",
        compiler_params=LIMIT,
    )(here(came))


def spread_sum_kernel(scaling, came_ref, copies_ref):
    total = jnp.sum(came_ref[...].astype(F32), axis=0)
    if scaling is not None:
        total = total * scaling
    total = total.astype(BF)
    for i in range(copies_ref.shape[0]):
        copies_ref[i] = total


def spread_sum(came, scaling, copies):
    return pl.pallas_call(
        functools.partial(spread_sum_kernel, scaling),
        out_shape=pltpu.VMEM((copies, *came.shape[1:]), BF),
        compiler_params=LIMIT,
    )(here(came))


def untile_kernel(tiles_ref, copies_ref):
    rows, width = copies_ref.shape[1:]
    columns = width // LANES
    for n in range(rows // TILE * columns):
        row, lane = n // columns * TILE, n % columns * LANES
        tile = tiles_ref[n]
        for i in range(copies_ref.shape[0]):
            copies_ref[i, row : row + TILE, lane : lane + LANES] = tile


def untile(tiles, shape):
    return pl.pallas_call(
        untile_kernel, out_shape=pltpu.VMEM(shape, BF), name="untile", compiler_params=LIMIT
    )(here(tiles))


def unpack_kernel(own_ref, other_ref, conv_ref, attn_ref, sem):
    conv_rows = conv_ref.shape[2]
    mine = lax.axis_index(PAIR)
    moves = []
    for n, (ref, half) in enumerate(((own_ref, mine), (other_ref, 1 - mine))):
        moves.append(
            pltpu.make_async_copy(ref.at[:, 0:conv_rows], conv_ref.at[half], sem.at[n, 0])
        )
        moves.append(
            pltpu.make_async_copy(ref.at[:, conv_rows:], attn_ref.at[half], sem.at[n, 1])
        )
    for move in moves:
        move.start()
    for move in moves:
        move.wait()


def unpack(own, other, conv_rows, attn_rows):
    near, _, width = own.shape
    return pl.pallas_call(
        unpack_kernel,
        out_shape=(
            jax.ShapeDtypeStruct((2, near, conv_rows // (2 * near), width), BF),
            jax.ShapeDtypeStruct((2, near, attn_rows // (2 * near), width), BF),
        ),
        in_specs=[pl.BlockSpec(memory_space=pltpu.VMEM)] * 2,
        out_specs=[pl.BlockSpec(memory_space=pl.ANY)] * 2,
        scratch_shapes=[pltpu.SemaphoreType.DMA((2, 2))],
        name="unpack",
        compiler_params=LIMIT,
    )(here(own), here(other))


def exchange(values, axis):
    return lax.all_to_all(values, axis, 0, 0, tiled=True)


def far_off(values):
    return pltpu.with_memory_space_constraint(values, pltpu.HBM)


def here(values):
    return pltpu.with_memory_space_constraint(values, pltpu.VMEM)


def patch_swaps(outer, inner):
    count = lax.axis_size(VERT)
    steps = [(i, i + 1) for i in range(1, count - 1, 2)]
    from_outer = lax.ppermute(outer, VERT, steps + [(b, a) for a, b in steps])
    from_inner = swap(inner)
    return from_outer, from_inner


def swap(values):
    return lax.ppermute(values, PAIR, [(0, 1), (1, 0)])


def body(frames, cotangent, table, w_conv, w_attn):
    _, patch, _ = frames.shape
    parts = lax.axis_size(TM)
    patches = lax.axis_size(VERT)
    near = lax.axis_size(NEAR)
    core = lax.axis_index(PAIR)
    low, high = frames[:, :HW], frames[:, patch - HW :]
    outer, inner = patch_swaps(
        jnp.where(core == 0, low, high), jnp.where(core == 0, high, low)
    )
    frames, cotangent, table, w_conv, picks = stage(frames, cotangent, table.T, w_conv)
    sent, pre, gathered = conv_forward(
        frames, cotangent, outer, inner, picks, w_conv, parts
    )
    back_time, attn_parts = attention(exchange(sent, TM), w_attn)
    back = exchange(back_time, TM)
    local, rim_outer, rim_inner, kept, given = conv_backward(
        back, pre, gathered, table, w_conv, attn_parts, near
    )
    came = swap(given)
    outer, inner = patch_swaps(rim_outer, rim_inner)
    weights = pair_sum(kept, came)
    low, high = jnp.where(core == 0, outer, inner), jnp.where(core == 0, inner, outer)
    arrived = jnp.concatenate([low, high], axis=1).astype(F32)
    grad_frames = (local + arrived).astype(BF)
    count = weights[0].size // (TILE * LANES)
    line, plane = lax.axis_size(LINE), lax.axis_size(PLANE)
    each = -(-count // line)
    came = exchange(weights, NEAR)
    tiles = first_sum(came, each * line)
    came = exchange(tiles, LINE).reshape(line, each, TILE, LANES)
    copies = spread_sum(came, None, plane)
    came = exchange(copies, PLANE)
    scaling = 1.0 / math.sqrt(TF * patch * patches)
    copies = spread_sum(came, scaling, line).reshape(tiles.shape)
    copies = untile(exchange(copies, LINE), weights.shape)
    own = exchange(copies, NEAR)
    grad_conv, grad_attn = unpack(own, swap(own), w_conv.shape[0], attn_parts.shape[0])
    return grad_frames, grad_conv.reshape(w_conv.shape), grad_attn.reshape(w_attn.shape)


def solution(mesh):
    parts, patches = mesh.devices.shape
    sizes = (parts // 4, 2, 2, patches // 16, 2, 2, 2, 2)
    fine = jax.sharding.Mesh(mesh.devices.reshape(sizes), TM + VERT)
    return jax.shard_map(
        body,
        mesh=fine,
        in_specs=(P(TM, VERT, None), P(TM, VERT, None), P(VERT, None), P(), P()),
        out_specs=(P(TM, VERT, None), P(), P()),
        check_vma=False,
    )
```

```python
import functools
import math

import jax
import jax.numpy as jnp
from jax import lax
from jax.experimental import pallas as pl
from jax.experimental.pallas import tpu as pltpu
from jax.sharding import PartitionSpec as P


TF = 16
HEADS = 8
HW = 64
TM = ("x_hi", "x_lo", "z_hi")
VERT = ("y_hi", "y_lo", "z_mid", "z_lo", "core")
PAIR = "core"
NEAR = ("x_lo", "y_lo", "z_lo")
LINE = ("z_hi", "z_mid")
PLANE = ("x_hi", "y_hi")
TILE = 16
BF = jnp.bfloat16
F32 = jnp.float32

LIMIT = pltpu.CompilerParams(vmem_limit_bytes=32 * 1024 * 1024)


def mm(left, right):
    return jnp.dot(left, right, preferred_element_type=F32)


def mm_nt(left, right):
    return lax.dot_general(left, right, (((1,), (1,)), ((), ())), preferred_element_type=F32)


def mm_tn(left, right):
    return lax.dot_general(left, right, (((0,), (0,)), ((), ())), preferred_element_type=F32)


def slot_places(table):
    lanes = lax.broadcasted_iota(jnp.int32, table.shape, 1)
    return jnp.where(table < 0, -1, table - table[0:1] + lanes + HW).astype(F32)


def stage_kernel(
    frames_ref, cot_ref, table_ref, w_ref, frames_out, cot_out, table_out, w_out, picks_ref, sem
):
    pairs = (
        (table_ref, table_out),
        (w_ref, w_out),
        (frames_ref, frames_out),
        (cot_ref, cot_out),
    )
    moves = [pltpu.make_async_copy(a, b, sem.at[i]) for i, (a, b) in enumerate(pairs)]
    for move in moves:
        move.start()
    moves[0].wait()
    stencil, patch = table_out.shape
    places = slot_places(table_out[...])
    row = lax.broadcasted_iota(jnp.int32, (patch, patch), 0)
    square = jnp.full((patch, patch), -1.0, F32)
    for j in range(1, stencil):
        square = jnp.where(row == j, places[j : j + 1], square)
    columns = square.T
    lanes = lax.broadcasted_iota(jnp.int32, (patch, patch + 2 * HW), 1).astype(F32)
    for j in range(1, stencil):
        picks_ref[(j - 1) * patch : j * patch, :] = jnp.where(
            lanes == columns[:, j : j + 1], 1.0, 0.0
        ).astype(BF)
    for move in moves[1:]:
        move.wait()


def stage(frames, cotangent, table, w_conv):
    stencil, patch = table.shape
    return pl.pallas_call(
        stage_kernel,
        out_shape=(
            pltpu.VMEM(frames.shape, BF),
            pltpu.VMEM(cotangent.shape, BF),
            pltpu.VMEM(table.shape, jnp.int32),
            pltpu.VMEM(w_conv.shape, BF),
            pltpu.VMEM(((stencil - 1) * patch, patch + 2 * HW), BF),
        ),
        in_specs=[pl.BlockSpec(memory_space=pl.ANY)] * 4,
        scratch_shapes=[pltpu.SemaphoreType.DMA((4,))],
        name="stage",
        compiler_params=LIMIT,
    )(*(far_off(x) for x in (frames, cotangent, table, w_conv)))


def conv_forward_kernel(
    frames_ref, cot_ref, outer_ref, inner_ref, picks_ref, w_ref, sent_ref, pre_ref, gathered_ref
):
    frames_here, patch, width = frames_ref.shape
    stencil = picks_ref.shape[0] // patch + 1
    group = sent_ref.shape[3]
    first = lax.axis_index(PAIR) == 0
    for t in range(frames_here):
        rows = pl.ds(t * patch, patch)
        low = jnp.where(first, outer_ref[t], inner_ref[t])
        high = jnp.where(first, inner_ref[t], outer_ref[t])
        extended = jnp.concatenate([low, frames_ref[t], high], axis=0)
        taken = mm(picks_ref[...], extended).astype(BF)
        gathered_ref[rows, 0:width] = frames_ref[t]
        for j in range(1, stencil):
            gathered_ref[rows, j * width : (j + 1) * width] = taken[(j - 1) * patch : j * patch]
        pre = mm(gathered_ref[rows, :], w_ref[...])
        pre_ref[rows, :] = pre
        gate = jax.nn.sigmoid(pre)
        hidden = (frames_ref[t].astype(F32) + pre * gate).astype(BF)
        for i in range(patch // group):
            sent_ref[i, 0, t] = hidden[i * group : (i + 1) * group]
            sent_ref[i, 1, t] = cot_ref[t, i * group : (i + 1) * group]


def conv_forward(frames, cotangent, outer, inner, picks, w_conv, parts):
    frames_here, patch, width = frames.shape
    rows = frames_here * patch
    return pl.pallas_call(
        conv_forward_kernel,
        out_shape=(
            pltpu.VMEM((parts, 2, frames_here, patch // parts, width), BF),
            pltpu.VMEM((rows, width), F32),
            pltpu.VMEM((rows, w_conv.shape[0]), BF),
        ),
        name="conv_forward",
        compiler_params=LIMIT,
    )(here(frames), here(cotangent), here(outer), here(inner), here(picks), here(w_conv))


def attention_kernel(came_ref, w_ref, back_ref, parts_ref):
    parts, _, frames_here, group, width = came_ref.shape
    frames_all = parts * frames_here
    rows_all = frames_all * group
    head_dim = width // HEADS
    scaling = head_dim ** (-0.5)
    half = 8
    rows = frames_all * half
    hidden = came_ref[:, 0].reshape(rows_all, width)
    grads = came_ref[:, 1].reshape(rows_all, width)

    def halves(values):
        cube = values.reshape(frames_all, group, width)
        return [cube[:, s : s + half].reshape(rows, width) for s in range(0, group, half)]

    query = halves(mm(hidden, w_ref[0]))
    key = halves(mm(hidden, w_ref[1]))
    value = halves(mm(hidden, w_ref[2]))
    grad_out = halves(mm_nt(grads, w_ref[3]))
    lane_head = lax.broadcasted_iota(jnp.int32, (rows, width), 1) // head_dim
    same = (
        lax.broadcasted_iota(jnp.int32, (rows, rows), 0) % half
        == lax.broadcasted_iota(jnp.int32, (rows, rows), 1) % half
    )
    same = jnp.where(same, 1.0, 0.0).astype(F32).reshape(1, frames_all, half, rows)

    def spread(values):
        return jnp.concatenate(
            [jnp.where(lane_head == h, values, 0.0).astype(BF) for h in range(HEADS)], axis=0
        )

    def collect(values):
        total = jnp.where(lane_head == 0, values[0:rows], 0.0)
        for h in range(1, HEADS):
            total = jnp.where(lane_head == h, values[h * rows : (h + 1) * rows], total)
        return total

    results = []
    for q32, k32, v32, g32 in zip(query, key, value, grad_out):
        q, g = q32.astype(BF), g32.astype(BF)
        k_heads, v_heads = spread(k32), spread(v32)
        shape4 = (HEADS, frames_all, half, rows)
        scores = mm_nt(k_heads, q).reshape(shape4) * scaling
        expo = jnp.exp(scores - jnp.max(scores, axis=1, keepdims=True))
        probs = expo * (same / jnp.sum(expo, axis=1, keepdims=True))
        probs_b = probs.reshape(-1, rows).astype(BF)
        grad_probs = mm_nt(v_heads, g).reshape(shape4)
        inner = jnp.sum(probs * grad_probs, axis=1, keepdims=True)
        grad_scores = (scaling * probs * (grad_probs - inner)).reshape(-1, rows).astype(BF)
        results.append(
            (
                mm_tn(probs_b, v_heads),
                mm_tn(grad_scores, k_heads),
                collect(mm(grad_scores, q)),
                collect(mm(probs_b, g)),
            )
        )

    def joined(index):
        pieces = [r[index].reshape(frames_all, half, width) for r in results]
        return jnp.concatenate(pieces, axis=1).reshape(rows_all, width).astype(BF)

    attended, grad_query, grad_key, grad_value = (joined(i) for i in range(4))
    back = (
        grads.astype(F32)
        + mm_nt(grad_query, w_ref[0])
        + mm_nt(grad_key, w_ref[1])
        + mm_nt(grad_value, w_ref[2])
    )
    back_ref[...] = back.astype(BF).reshape(back_ref.shape)
    parts_ref[0:width] = mm_tn(hidden, grad_query).astype(parts_ref.dtype)
    parts_ref[1 * width : 2 * width] = mm_tn(hidden, grad_key).astype(parts_ref.dtype)
    parts_ref[2 * width : 3 * width] = mm_tn(hidden, grad_value).astype(parts_ref.dtype)
    parts_ref[3 * width : 4 * width] = mm_tn(attended, grads).astype(parts_ref.dtype)


def attention(came, w_attn):
    parts, _, frames_here, group, width = came.shape
    return pl.pallas_call(
        attention_kernel,
        out_shape=(
            pltpu.VMEM((parts, frames_here, group, width), BF),
            pltpu.VMEM((4 * width, width), BF),
        ),
        name="attention",
        compiler_params=LIMIT,
    )(here(came), w_attn)


def conv_backward_kernel(
    back_ref,
    pre_ref,
    gathered_ref,
    table_ref,
    w_ref,
    attn_ref,
    local_ref,
    outer_ref,
    inner_ref,
    kept_ref,
    given_ref,
):
    parts, frames_here, group, width = back_ref.shape
    patch = parts * group
    stencil = table_ref.shape[0]
    places = slot_places(table_ref[...])
    target = lax.broadcasted_iota(jnp.int32, (patch + 2 * HW, patch), 0).astype(F32)
    puts = jnp.concatenate(
        [jnp.where(target == places[j : j + 1], 1.0, 0.0).astype(BF) for j in range(stencil)],
        axis=1,
    )
    pre = pre_ref[...]
    gate = jax.nn.sigmoid(pre)
    slope = gate * (1.0 + pre * (1.0 - gate))
    first = lax.axis_index(PAIR) == 0
    backs, grads = [], []
    for t in range(frames_here):
        back = jnp.concatenate([back_ref[i, t] for i in range(parts)], axis=0).astype(F32)
        backs.append(back)
        grads.append((back * slope[t * patch : (t + 1) * patch]).astype(BF))
    for t in range(frames_here):
        spread = mm_nt(grads[t], w_ref[...]).astype(BF)
        stacked = jnp.concatenate(
            [spread[:, j * width : (j + 1) * width] for j in range(stencil)], axis=0
        )
        extended = mm(puts, stacked)
        low, high = extended[0:HW].astype(BF), extended[patch + HW :].astype(BF)
        outer_ref[t] = jnp.where(first, low, high)
        inner_ref[t] = jnp.where(first, high, low)
        local_ref[t] = backs[t] + extended[HW : HW + patch]
    grad_pre = jnp.concatenate(grads, axis=0)
    grad_w = mm_tn(gathered_ref[...], grad_pre).astype(BF)
    near = kept_ref.shape[0]
    conv_rows = grad_w.shape[0] // (2 * near)
    attn_rows = attn_ref.shape[0] // (2 * near)
    for i in range(near):
        for source, rows, start in ((grad_w, conv_rows, 0), (attn_ref, attn_rows, conv_rows)):
            lower = source[i * rows : (i + 1) * rows]
            upper = source[(near + i) * rows : (near + i + 1) * rows]
            kept_ref[i, start : start + rows] = jnp.where(first, lower, upper)
            given_ref[i, start : start + rows] = jnp.where(first, upper, lower)


def conv_backward(back, pre, gathered, table, w_conv, attn_parts, near):
    parts, frames_here, group, width = back.shape
    patch = parts * group
    weight_rows = (w_conv.shape[0] + attn_parts.shape[0]) // (2 * near)
    return pl.pallas_call(
        conv_backward_kernel,
        out_shape=(
            pltpu.VMEM((frames_here, patch, width), F32),
            pltpu.VMEM((frames_here, HW, width), BF),
            pltpu.VMEM((frames_here, HW, width), BF),
            pltpu.VMEM((near, weight_rows, width), BF),
            pltpu.VMEM((near, weight_rows, width), BF),
        ),
        name="conv_backward",
        compiler_params=LIMIT,
    )(here(back), here(pre), here(gathered), here(table), here(w_conv), here(attn_parts))


LANES = 128


def pair_sum_kernel(kept_ref, came_ref, sum_ref):
    sum_ref[...] = (kept_ref[...].astype(F32) + came_ref[...].astype(F32)).astype(BF)


def pair_sum(kept, came):
    return pl.pallas_call(
        pair_sum_kernel,
        out_shape=pltpu.VMEM(kept.shape, BF),
        name="pair_sum",
        compiler_params=LIMIT,
    )(here(kept), here(came))


def first_sum_kernel(came_ref, tiles_ref):
    total = came_ref[0].astype(F32)
    for i in range(1, came_ref.shape[0]):
        total = total + came_ref[i].astype(F32)
    total = total.astype(BF)
    columns = total.shape[1] // LANES
    count = total.shape[0] // TILE * columns
    for n in range(count):
        row, lane = n // columns * TILE, n % columns * LANES
        tiles_ref[n] = total[row : row + TILE, lane : lane + LANES]
    rest = tiles_ref.shape[0] - count
    if rest:
        tiles_ref[count:] = jnp.zeros((rest, TILE, LANES), BF)


def first_sum(came, tiles):
    return pl.pallas_call(
        first_sum_kernel,
        out_shape=pltpu.VMEM((tiles, TILE, LANES), BF),
        name="first_sum",
        compiler_params=LIMIT,
    )(here(came))


def spread_sum_kernel(scaling, came_ref, copies_ref):
    total = jnp.sum(came_ref[...].astype(F32), axis=0)
    if scaling is not None:
        total = total * scaling
    total = total.astype(BF)
    for i in range(copies_ref.shape[0]):
        copies_ref[i] = total


def spread_sum(came, scaling, copies):
    return pl.pallas_call(
        functools.partial(spread_sum_kernel, scaling),
        out_shape=pltpu.VMEM((copies, *came.shape[1:]), BF),
        compiler_params=LIMIT,
    )(here(came))


def untile_kernel(tiles_ref, copies_ref):
    rows, width = copies_ref.shape[1:]
    columns = width // LANES
    for n in range(rows // TILE * columns):
        row, lane = n // columns * TILE, n % columns * LANES
        tile = tiles_ref[n]
        for i in range(copies_ref.shape[0]):
            copies_ref[i, row : row + TILE, lane : lane + LANES] = tile


def untile(tiles, shape):
    return pl.pallas_call(
        untile_kernel, out_shape=pltpu.VMEM(shape, BF), name="untile", compiler_params=LIMIT
    )(here(tiles))


def unpack_half(half_ref, conv_ref, attn_ref, half, sem):
    conv_rows = conv_ref.shape[2]
    moves = [
        pltpu.make_async_copy(half_ref.at[:, 0:conv_rows], conv_ref.at[half], sem.at[0]),
        pltpu.make_async_copy(half_ref.at[:, conv_rows:], attn_ref.at[half], sem.at[1]),
    ]
    for move in moves:
        move.start()
    for move in moves:
        move.wait()


def unpack_own_kernel(own_ref, conv_ref, attn_ref, sem):
    unpack_half(own_ref, conv_ref, attn_ref, lax.axis_index(PAIR), sem)


def unpack_other_kernel(other_ref, conv_in, attn_in, conv_ref, attn_ref, sem):
    unpack_half(other_ref, conv_ref, attn_ref, 1 - lax.axis_index(PAIR), sem)


def unpack_own(own, conv_rows, attn_rows):
    near, _, width = own.shape
    return pl.pallas_call(
        unpack_own_kernel,
        out_shape=(
            jax.ShapeDtypeStruct((2, near, conv_rows // (2 * near), width), BF),
            jax.ShapeDtypeStruct((2, near, attn_rows // (2 * near), width), BF),
        ),
        in_specs=[pl.BlockSpec(memory_space=pltpu.VMEM)],
        out_specs=[pl.BlockSpec(memory_space=pl.ANY)] * 2,
        scratch_shapes=[pltpu.SemaphoreType.DMA((2,))],
        name="unpack_own",
        compiler_params=LIMIT,
    )(here(own))


def unpack_other(other, conv, attn):
    return pl.pallas_call(
        unpack_other_kernel,
        out_shape=(
            jax.ShapeDtypeStruct(conv.shape, BF),
            jax.ShapeDtypeStruct(attn.shape, BF),
        ),
        in_specs=[pl.BlockSpec(memory_space=pltpu.VMEM)] + [pl.BlockSpec(memory_space=pl.ANY)] * 2,
        out_specs=[pl.BlockSpec(memory_space=pl.ANY)] * 2,
        scratch_shapes=[pltpu.SemaphoreType.DMA((2,))],
        input_output_aliases={1: 0, 2: 1},
        name="unpack_other",
        compiler_params=LIMIT,
    )(here(other), conv, attn)


def exchange(values, axis):
    return lax.all_to_all(values, axis, 0, 0, tiled=True)


def far_off(values):
    return pltpu.with_memory_space_constraint(values, pltpu.HBM)


def here(values):
    return pltpu.with_memory_space_constraint(values, pltpu.VMEM)


def patch_swaps(outer, inner):
    count = lax.axis_size(VERT)
    steps = [(i, i + 1) for i in range(1, count - 1, 2)]
    from_outer = lax.ppermute(outer, VERT, steps + [(b, a) for a, b in steps])
    from_inner = swap(inner)
    return from_outer, from_inner


def swap(values):
    return lax.ppermute(values, PAIR, [(0, 1), (1, 0)])


def body(frames, cotangent, table, w_conv, w_attn):
    _, patch, _ = frames.shape
    parts = lax.axis_size(TM)
    patches = lax.axis_size(VERT)
    near = lax.axis_size(NEAR)
    core = lax.axis_index(PAIR)
    low, high = frames[:, :HW], frames[:, patch - HW :]
    outer, inner = patch_swaps(
        jnp.where(core == 0, low, high), jnp.where(core == 0, high, low)
    )
    frames, cotangent, table, w_conv, picks = stage(frames, cotangent, table.T, w_conv)
    sent, pre, gathered = conv_forward(
        frames, cotangent, outer, inner, picks, w_conv, parts
    )
    back_time, attn_parts = attention(exchange(sent, TM), w_attn)
    back = exchange(back_time, TM)
    local, rim_outer, rim_inner, kept, given = conv_backward(
        back, pre, gathered, table, w_conv, attn_parts, near
    )
    came = swap(given)
    outer, inner = patch_swaps(rim_outer, rim_inner)
    weights = pair_sum(kept, came)
    low, high = jnp.where(core == 0, outer, inner), jnp.where(core == 0, inner, outer)
    arrived = jnp.concatenate([low, high], axis=1).astype(F32)
    grad_frames = (local + arrived).astype(BF)
    count = weights[0].size // (TILE * LANES)
    line, plane = lax.axis_size(LINE), lax.axis_size(PLANE)
    each = -(-count // line)
    came = exchange(weights, NEAR)
    tiles = first_sum(came, each * line)
    came = exchange(tiles, LINE).reshape(line, each, TILE, LANES)
    copies = spread_sum(came, None, plane)
    came = exchange(copies, PLANE)
    scaling = 1.0 / math.sqrt(TF * patch * patches)
    copies = spread_sum(came, scaling, line).reshape(tiles.shape)
    copies = untile(exchange(copies, LINE), weights.shape)
    own = exchange(copies, NEAR)
    other = swap(own)
    grad_conv, grad_attn = unpack_other(
        other, *unpack_own(own, w_conv.shape[0], attn_parts.shape[0])
    )
    return grad_frames, grad_conv.reshape(w_conv.shape), grad_attn.reshape(w_attn.shape)


def solution(mesh):
    parts, patches = mesh.devices.shape
    sizes = (parts // 4, 2, 2, patches // 16, 2, 2, 2, 2)
    fine = jax.sharding.Mesh(mesh.devices.reshape(sizes), TM + VERT)
    return jax.shard_map(
        body,
        mesh=fine,
        in_specs=(P(TM, VERT, None), P(TM, VERT, None), P(VERT, None), P(), P()),
        out_specs=(P(TM, VERT, None), P(), P()),
        check_vma=False,
    )
```

```python
import functools
import math

import jax
import jax.numpy as jnp
from jax import lax
from jax.experimental import pallas as pl
from jax.experimental.pallas import tpu as pltpu
from jax.sharding import PartitionSpec as P


TF = 16
HEADS = 8
HW = 64
TM = ("x_hi", "x_lo", "z_hi")
VERT = ("y_hi", "y_lo", "z_mid", "z_lo", "core")
PAIR = "core"
NEAR = ("x_lo", "y_lo", "z_lo")
LINE = ("z_hi", "z_mid")
PLANE = ("x_hi", "y_hi")
TILE = 16
BF = jnp.bfloat16
F32 = jnp.float32

LIMIT = pltpu.CompilerParams(vmem_limit_bytes=32 * 1024 * 1024)


def mm(left, right):
    return jnp.dot(left, right, preferred_element_type=F32)


def mm_nt(left, right):
    return lax.dot_general(left, right, (((1,), (1,)), ((), ())), preferred_element_type=F32)


def mm_tn(left, right):
    return lax.dot_general(left, right, (((0,), (0,)), ((), ())), preferred_element_type=F32)


def slot_places(table):
    lanes = lax.broadcasted_iota(jnp.int32, table.shape, 1)
    return jnp.where(table < 0, -1, table - table[0:1] + lanes + HW).astype(F32)


def stage_kernel(
    frames_ref, cot_ref, table_ref, w_ref, frames_out, cot_out, table_out, w_out, picks_ref, sem
):
    pairs = (
        (table_ref, table_out),
        (w_ref, w_out),
        (frames_ref, frames_out),
        (cot_ref, cot_out),
    )
    moves = [pltpu.make_async_copy(a, b, sem.at[i]) for i, (a, b) in enumerate(pairs)]
    for move in moves:
        move.start()
    moves[0].wait()
    stencil, patch = table_out.shape
    places = slot_places(table_out[...])
    row = lax.broadcasted_iota(jnp.int32, (patch, patch), 0)
    square = jnp.full((patch, patch), -1.0, F32)
    for j in range(1, stencil):
        square = jnp.where(row == j, places[j : j + 1], square)
    columns = square.T
    lanes = lax.broadcasted_iota(jnp.int32, (patch, patch + 2 * HW), 1).astype(F32)
    for j in range(1, stencil):
        picks_ref[(j - 1) * patch : j * patch, :] = jnp.where(
            lanes == columns[:, j : j + 1], 1.0, 0.0
        ).astype(BF)
    for move in moves[1:]:
        move.wait()


def stage(frames, cotangent, table, w_conv):
    stencil, patch = table.shape
    return pl.pallas_call(
        stage_kernel,
        out_shape=(
            pltpu.VMEM(frames.shape, BF),
            pltpu.VMEM(cotangent.shape, BF),
            pltpu.VMEM(table.shape, jnp.int32),
            pltpu.VMEM(w_conv.shape, BF),
            pltpu.VMEM(((stencil - 1) * patch, patch + 2 * HW), BF),
        ),
        in_specs=[pl.BlockSpec(memory_space=pl.ANY)] * 4,
        scratch_shapes=[pltpu.SemaphoreType.DMA((4,))],
        name="stage",
        compiler_params=LIMIT,
    )(*(far_off(x) for x in (frames, cotangent, table, w_conv)))


def conv_forward_kernel(
    frames_ref, cot_ref, outer_ref, inner_ref, picks_ref, w_ref, sent_ref, pre_ref, gathered_ref
):
    frames_here, patch, width = frames_ref.shape
    stencil = picks_ref.shape[0] // patch + 1
    group = sent_ref.shape[3]
    first = lax.axis_index(PAIR) == 0
    for t in range(frames_here):
        rows = pl.ds(t * patch, patch)
        low = jnp.where(first, outer_ref[t], inner_ref[t])
        high = jnp.where(first, inner_ref[t], outer_ref[t])
        extended = jnp.concatenate([low, frames_ref[t], high], axis=0)
        taken = mm(picks_ref[...], extended).astype(BF)
        gathered_ref[rows, 0:width] = frames_ref[t]
        for j in range(1, stencil):
            gathered_ref[rows, j * width : (j + 1) * width] = taken[(j - 1) * patch : j * patch]
        pre = mm(gathered_ref[rows, :], w_ref[...])
        pre_ref[rows, :] = pre
        gate = jax.nn.sigmoid(pre)
        hidden = (frames_ref[t].astype(F32) + pre * gate).astype(BF)
        for i in range(patch // group):
            sent_ref[i, 0, t] = hidden[i * group : (i + 1) * group]
            sent_ref[i, 1, t] = cot_ref[t, i * group : (i + 1) * group]


def conv_forward(frames, cotangent, outer, inner, picks, w_conv, parts):
    frames_here, patch, width = frames.shape
    rows = frames_here * patch
    return pl.pallas_call(
        conv_forward_kernel,
        out_shape=(
            pltpu.VMEM((parts, 2, frames_here, patch // parts, width), BF),
            pltpu.VMEM((rows, width), F32),
            pltpu.VMEM((rows, w_conv.shape[0]), BF),
        ),
        name="conv_forward",
        compiler_params=LIMIT,
    )(here(frames), here(cotangent), here(outer), here(inner), here(picks), here(w_conv))


def attention_kernel(came_ref, w_ref, back_ref, parts_ref):
    parts, _, frames_here, group, width = came_ref.shape
    frames_all = parts * frames_here
    rows_all = frames_all * group
    head_dim = width // HEADS
    scaling = head_dim ** (-0.5)
    half = 8
    rows = frames_all * half
    hidden = came_ref[:, 0].reshape(rows_all, width)
    grads = came_ref[:, 1].reshape(rows_all, width)

    def halves(values):
        cube = values.reshape(frames_all, group, width)
        return [cube[:, s : s + half].reshape(rows, width) for s in range(0, group, half)]

    query = halves(mm(hidden, w_ref[0]))
    key = halves(mm(hidden, w_ref[1]))
    value = halves(mm(hidden, w_ref[2]))
    grad_out = halves(mm_nt(grads, w_ref[3]))
    lane_head = lax.broadcasted_iota(jnp.int32, (rows, width), 1) // head_dim
    same = (
        lax.broadcasted_iota(jnp.int32, (rows, rows), 0) % half
        == lax.broadcasted_iota(jnp.int32, (rows, rows), 1) % half
    )
    same = jnp.where(same, 1.0, 0.0).astype(F32).reshape(1, frames_all, half, rows)

    def spread(values):
        return jnp.concatenate(
            [jnp.where(lane_head == h, values, 0.0).astype(BF) for h in range(HEADS)], axis=0
        )

    def collect(values):
        total = jnp.where(lane_head == 0, values[0:rows], 0.0)
        for h in range(1, HEADS):
            total = jnp.where(lane_head == h, values[h * rows : (h + 1) * rows], total)
        return total

    results = []
    for q32, k32, v32, g32 in zip(query, key, value, grad_out):
        q, g = q32.astype(BF), g32.astype(BF)
        k_heads, v_heads = spread(k32), spread(v32)
        shape4 = (HEADS, frames_all, half, rows)
        scores = mm_nt(k_heads, q).reshape(shape4) * scaling
        expo = jnp.exp(scores - jnp.max(scores, axis=1, keepdims=True))
        probs = expo * (same / jnp.sum(expo, axis=1, keepdims=True))
        probs_b = probs.reshape(-1, rows).astype(BF)
        grad_probs = mm_nt(v_heads, g).reshape(shape4)
        inner = jnp.sum(probs * grad_probs, axis=1, keepdims=True)
        grad_scores = (scaling * probs * (grad_probs - inner)).reshape(-1, rows).astype(BF)
        results.append(
            (
                mm_tn(probs_b, v_heads),
                mm_tn(grad_scores, k_heads),
                collect(mm(grad_scores, q)),
                collect(mm(probs_b, g)),
            )
        )

    def joined(index):
        pieces = [r[index].reshape(frames_all, half, width) for r in results]
        return jnp.concatenate(pieces, axis=1).reshape(rows_all, width).astype(BF)

    attended, grad_query, grad_key, grad_value = (joined(i) for i in range(4))
    back = (
        grads.astype(F32)
        + mm_nt(grad_query, w_ref[0])
        + mm_nt(grad_key, w_ref[1])
        + mm_nt(grad_value, w_ref[2])
    )
    back_ref[...] = back.astype(BF).reshape(back_ref.shape)
    parts_ref[0:width] = mm_tn(hidden, grad_query).astype(parts_ref.dtype)
    parts_ref[1 * width : 2 * width] = mm_tn(hidden, grad_key).astype(parts_ref.dtype)
    parts_ref[2 * width : 3 * width] = mm_tn(hidden, grad_value).astype(parts_ref.dtype)
    parts_ref[3 * width : 4 * width] = mm_tn(attended, grads).astype(parts_ref.dtype)


def attention(came, w_attn):
    parts, _, frames_here, group, width = came.shape
    return pl.pallas_call(
        attention_kernel,
        out_shape=(
            pltpu.VMEM((parts, frames_here, group, width), BF),
            pltpu.VMEM((4 * width, width), BF),
        ),
        name="attention",
        compiler_params=LIMIT,
    )(here(came), w_attn)


def conv_backward_kernel(
    back_ref,
    pre_ref,
    gathered_ref,
    table_ref,
    w_ref,
    attn_ref,
    local_ref,
    outer_ref,
    kept_ref,
    given_ref,
):
    parts, frames_here, group, width = back_ref.shape
    patch = parts * group
    stencil = table_ref.shape[0]
    places = slot_places(table_ref[...])
    target = lax.broadcasted_iota(jnp.int32, (patch + 2 * HW, patch), 0).astype(F32)
    puts = jnp.concatenate(
        [jnp.where(target == places[j : j + 1], 1.0, 0.0).astype(BF) for j in range(stencil)],
        axis=1,
    )
    pre = pre_ref[...]
    gate = jax.nn.sigmoid(pre)
    slope = gate * (1.0 + pre * (1.0 - gate))
    first = lax.axis_index(PAIR) == 0
    backs, grads, inner = [], [], []
    for t in range(frames_here):
        back = jnp.concatenate([back_ref[i, t] for i in range(parts)], axis=0).astype(F32)
        backs.append(back)
        grads.append((back * slope[t * patch : (t + 1) * patch]).astype(BF))
    for t in range(frames_here):
        spread = mm_nt(grads[t], w_ref[...]).astype(BF)
        stacked = jnp.concatenate(
            [spread[:, j * width : (j + 1) * width] for j in range(stencil)], axis=0
        )
        extended = mm(puts, stacked)
        low, high = extended[0:HW].astype(BF), extended[patch + HW :].astype(BF)
        outer_ref[t] = jnp.where(first, low, high)
        inner.append(jnp.where(first, high, low))
        local_ref[t] = backs[t] + extended[HW : HW + patch]
    grad_pre = jnp.concatenate(grads, axis=0)
    grad_w = mm_tn(gathered_ref[...], grad_pre).astype(BF)
    near = kept_ref.shape[0]
    inner = jnp.concatenate(inner, axis=0)
    conv_rows = grad_w.shape[0] // (2 * near)
    attn_rows = attn_ref.shape[0] // (2 * near)
    for i in range(near):
        for source, rows, start in ((grad_w, conv_rows, 0), (attn_ref, attn_rows, conv_rows)):
            lower = source[i * rows : (i + 1) * rows]
            upper = source[(near + i) * rows : (near + i + 1) * rows]
            kept_ref[i, start : start + rows] = jnp.where(first, lower, upper)
            given_ref[i, start : start + rows] = jnp.where(first, upper, lower)
        rim_rows = given_ref.shape[1] - kept_ref.shape[1]
        given_ref[i, kept_ref.shape[1] :] = inner[i * rim_rows : (i + 1) * rim_rows]


def conv_backward(back, pre, gathered, table, w_conv, attn_parts, near):
    parts, frames_here, group, width = back.shape
    patch = parts * group
    weight_rows = (w_conv.shape[0] + attn_parts.shape[0]) // (2 * near)
    return pl.pallas_call(
        conv_backward_kernel,
        out_shape=(
            pltpu.VMEM((frames_here, patch, width), F32),
            pltpu.VMEM((frames_here, HW, width), BF),
            pltpu.VMEM((near, weight_rows, width), BF),
            pltpu.VMEM((near, weight_rows + frames_here * HW // near, width), BF),
        ),
        name="conv_backward",
        compiler_params=LIMIT,
    )(here(back), here(pre), here(gathered), here(table), here(w_conv), here(attn_parts))


LANES = 128


def pair_sum_kernel(kept_ref, came_ref, sum_ref, rim_ref):
    near, rows, _ = kept_ref.shape
    sum_ref[...] = (kept_ref[...].astype(F32) + came_ref[:, 0:rows].astype(F32)).astype(BF)
    rim = jnp.concatenate([came_ref[i, rows:] for i in range(near)], axis=0)
    for t in range(rim_ref.shape[0]):
        rim_ref[t] = rim[t * HW : (t + 1) * HW]


def pair_sum(kept, came, frames_here):
    return pl.pallas_call(
        pair_sum_kernel,
        out_shape=(
            pltpu.VMEM(kept.shape, BF),
            pltpu.VMEM((frames_here, HW, kept.shape[2]), BF),
        ),
        name="pair_sum",
        compiler_params=LIMIT,
    )(here(kept), here(came))


def first_sum_kernel(came_ref, tiles_ref):
    total = came_ref[0].astype(F32)
    for i in range(1, came_ref.shape[0]):
        total = total + came_ref[i].astype(F32)
    total = total.astype(BF)
    columns = total.shape[1] // LANES
    count = total.shape[0] // TILE * columns
    for n in range(count):
        row, lane = n // columns * TILE, n % columns * LANES
        tiles_ref[n] = total[row : row + TILE, lane : lane + LANES]
    rest = tiles_ref.shape[0] - count
    if rest:
        tiles_ref[count:] = jnp.zeros((rest, TILE, LANES), BF)


def first_sum(came, tiles):
    return pl.pallas_call(
        first_sum_kernel,
        out_shape=pltpu.VMEM((tiles, TILE, LANES), BF),
        name="first_sum",
        compiler_params=LIMIT,
    )(here(came))


def spread_sum_kernel(scaling, came_ref, copies_ref):
    total = jnp.sum(came_ref[...].astype(F32), axis=0)
    if scaling is not None:
        total = total * scaling
    total = total.astype(BF)
    for i in range(copies_ref.shape[0]):
        copies_ref[i] = total


def spread_sum(came, scaling, copies):
    return pl.pallas_call(
        functools.partial(spread_sum_kernel, scaling),
        out_shape=pltpu.VMEM((copies, *came.shape[1:]), BF),
        compiler_params=LIMIT,
    )(here(came))


def untile_kernel(tiles_ref, copies_ref):
    rows, width = copies_ref.shape[1:]
    columns = width // LANES
    for n in range(rows // TILE * columns):
        row, lane = n // columns * TILE, n % columns * LANES
        tile = tiles_ref[n]
        for i in range(copies_ref.shape[0]):
            copies_ref[i, row : row + TILE, lane : lane + LANES] = tile


def untile(tiles, shape):
    return pl.pallas_call(
        untile_kernel, out_shape=pltpu.VMEM(shape, BF), name="untile", compiler_params=LIMIT
    )(here(tiles))


def unpack_kernel(own_ref, other_ref, conv_ref, attn_ref, sem):
    conv_rows = conv_ref.shape[2]
    mine = lax.axis_index(PAIR)
    moves = []
    for n, (ref, half) in enumerate(((own_ref, mine), (other_ref, 1 - mine))):
        moves.append(
            pltpu.make_async_copy(ref.at[:, 0:conv_rows], conv_ref.at[half], sem.at[n, 0])
        )
        moves.append(
            pltpu.make_async_copy(ref.at[:, conv_rows:], attn_ref.at[half], sem.at[n, 1])
        )
    for move in moves:
        move.start()
    for move in moves:
        move.wait()


def unpack(own, other, conv_rows, attn_rows):
    near, _, width = own.shape
    return pl.pallas_call(
        unpack_kernel,
        out_shape=(
            jax.ShapeDtypeStruct((2, near, conv_rows // (2 * near), width), BF),
            jax.ShapeDtypeStruct((2, near, attn_rows // (2 * near), width), BF),
        ),
        in_specs=[pl.BlockSpec(memory_space=pltpu.VMEM)] * 2,
        out_specs=[pl.BlockSpec(memory_space=pl.ANY)] * 2,
        scratch_shapes=[pltpu.SemaphoreType.DMA((2, 2))],
        name="unpack",
        compiler_params=LIMIT,
    )(here(own), here(other))


def exchange(values, axis):
    return lax.all_to_all(values, axis, 0, 0, tiled=True)


def far_off(values):
    return pltpu.with_memory_space_constraint(values, pltpu.HBM)


def here(values):
    return pltpu.with_memory_space_constraint(values, pltpu.VMEM)


def outer_swap(values):
    count = lax.axis_size(VERT)
    steps = [(i, i + 1) for i in range(1, count - 1, 2)]
    return lax.ppermute(values, VERT, steps + [(b, a) for a, b in steps])


def swap(values):
    return lax.ppermute(values, PAIR, [(0, 1), (1, 0)])


def body(frames, cotangent, table, w_conv, w_attn):
    frames_here, patch, _ = frames.shape
    parts = lax.axis_size(TM)
    patches = lax.axis_size(VERT)
    near = lax.axis_size(NEAR)
    core = lax.axis_index(PAIR)
    low, high = frames[:, :HW], frames[:, patch - HW :]
    outer = outer_swap(jnp.where(core == 0, low, high))
    inner = swap(jnp.where(core == 0, high, low))
    frames, cotangent, table, w_conv, picks = stage(frames, cotangent, table.T, w_conv)
    sent, pre, gathered = conv_forward(
        frames, cotangent, outer, inner, picks, w_conv, parts
    )
    back_time, attn_parts = attention(exchange(sent, TM), w_attn)
    back = exchange(back_time, TM)
    local, rim_outer, kept, given = conv_backward(
        back, pre, gathered, table, w_conv, attn_parts, near
    )
    came = swap(given)
    outer = outer_swap(rim_outer)
    weights, inner = pair_sum(kept, came, frames_here)
    low, high = jnp.where(core == 0, outer, inner), jnp.where(core == 0, inner, outer)
    arrived = jnp.concatenate([low, high], axis=1).astype(F32)
    grad_frames = (local + arrived).astype(BF)
    count = weights[0].size // (TILE * LANES)
    line, plane = lax.axis_size(LINE), lax.axis_size(PLANE)
    each = -(-count // line)
    came = exchange(weights, NEAR)
    tiles = first_sum(came, each * line)
    came = exchange(tiles, LINE).reshape(line, each, TILE, LANES)
    copies = spread_sum(came, None, plane)
    came = exchange(copies, PLANE)
    scaling = 1.0 / math.sqrt(TF * patch * patches)
    copies = spread_sum(came, scaling, line).reshape(tiles.shape)
    copies = untile(exchange(copies, LINE), weights.shape)
    own = exchange(copies, NEAR)
    grad_conv, grad_attn = unpack(own, swap(own), w_conv.shape[0], attn_parts.shape[0])
    return grad_frames, grad_conv.reshape(w_conv.shape), grad_attn.reshape(w_attn.shape)


def solution(mesh):
    parts, patches = mesh.devices.shape
    sizes = (parts // 4, 2, 2, patches // 16, 2, 2, 2, 2)
    fine = jax.sharding.Mesh(mesh.devices.reshape(sizes), TM + VERT)
    return jax.shard_map(
        body,
        mesh=fine,
        in_specs=(P(TM, VERT, None), P(TM, VERT, None), P(VERT, None), P(), P()),
        out_specs=(P(TM, VERT, None), P(), P()),
        check_vma=False,
    )
```
